256 devices in a mesh: grp: 8 (over x, z_lo), dev: 32 (over y, z_hi, core).
Axes of the slice: x: 4, y: 4, z: 8 (z_hi: 4, z_lo: 2; z = z_hi * 2 + z_lo), core: 2. Of those that a mesh axis runs over, the one named last changes fastest.
Arguments:
- query: bfloat16 [512, 128, 4096], P(('grp', 'dev')), may hold values from -100 to 100
- grad_out: bfloat16 [512, 128, 4096], P(('grp', 'dev')), may hold values from -6 to 6
- branch_kv: bfloat16 [512, 128, 1024], P(('grp', 'dev')), may hold values from -6 to 6
- root_kv: bfloat16 [1024, 1024], P('dev'), may hold values from -24 to 24
- lengths: int32 [512], P(('grp', 'dev')), may hold values from 0 to 128, as said below
- segments: int32 [512], P(('grp', 'dev')), may hold values from 0 to 3
Outputs:
- query_grad: bfloat16 [512, 128, 4096], P(('grp', 'dev'))
- branch_grad: bfloat16 [512, 128, 1024], P(('grp', 'dev'))
- root_grad: float32 [1024, 1024], P('dev')
The draws below stay inside these ranges and needn't reach their ends.
Inputs may be any that keep to these rules, and one draw needn't show every extreme that they name: `lengths`: A slot with length 0 holds no branch. A device's slots with live positions come before its empty slots. Within a group, device d and device d + 32/2 (d < 16) hold exactly 2 slots with live positions together; a quarter of a group's devices hold 2 such slots and a quarter hold none.
All inputs are finite; a program needn't handle non-finite values.
Results may differ from the reference program's by a relative error of at most 0.0069.
Values may be sent and summed in bfloat16 or wider, within the bound.
A program may use at most 128 MiB of HBM per device.

```python
import jax
import jax.numpy as jnp
from jax import lax

H = 32
KVH = 4
DH = 128
TILE = 128
R = 1024
SEGS = 4
TILES_DEV = 2
TILES = 512
N_GRP = 8
N_DEV = 32


def root_rows(key):
    drawn = jnp.clip(jax.random.normal(jax.random.fold_in(key, 11), (R, 2 * KVH * DH), jnp.float32), -6.0, 6.0)
    return drawn


def draw_root_kv(key, part):
    return root_rows(key).astype(jnp.bfloat16)


def draw_query(key, part):
    drawn = jnp.clip(jax.random.normal(jax.random.fold_in(key, 21), (TILES, TILE, H * DH), jnp.float32), -6.0, 6.0)
    return drawn.astype(jnp.bfloat16)


def draw_lengths(key, part):
    pairs = N_DEV // 2
    group_keys = jax.random.split(jax.random.fold_in(key, 31), N_GRP)

    def pattern(group_key):
        order_key, side_key = jax.random.split(group_key)
        order = jax.random.permutation(order_key, pairs)
        heavy = order < pairs // 2
        side = jax.random.randint(side_key, (pairs,), 0, 2)
        lower = jnp.where(heavy, 2 * side, 1)
        return jnp.concatenate([lower, 2 - lower])
    counts = jax.vmap(pattern)(group_keys).reshape(N_GRP * N_DEV)
    slots = jnp.arange(TILES_DEV)
    drawn = jax.random.randint(jax.random.fold_in(key, 32), (N_GRP * N_DEV, TILES_DEV), TILE // 4, TILE + 1)
    live = slots[None, :] < counts[:, None]
    return jnp.where(live, drawn, 0).reshape(TILES).astype(jnp.int32)


def place_ends(values, stream_key, smallest, top_value):
    dims = values.shape
    spot = [jax.random.randint(jax.random.fold_in(stream_key, axis), (), 0, dims[axis]) for axis in range(len(dims))]
    values = values.at[tuple(spot)].set(smallest)
    longest = dims.index(max(dims))
    spot[longest] = (spot[longest] + 1) % dims[longest]
    return values.at[tuple(spot)].set(top_value)


def steps_of(own_key, extent, pieces, least, high):
    factor_of, own = 1.0, jax.random.fold_in(own_key, 6)
    for axis_at, parts in pieces:
        draws = jnp.exp(jax.random.uniform(jax.random.fold_in(own, axis_at), (parts,), jnp.float32, least / len(pieces), high / len(pieces)))
        factor_of = factor_of * jnp.repeat(draws, extent[axis_at] // parts).reshape([-1 if axis == axis_at else 1 for axis in range(len(extent))])
    return factor_of


def gaussian(own_key, extent, spread, bound, cuts=(), held_as=jnp.bfloat16):
    result = jax.random.normal(own_key, extent, jnp.float32) * spread
    if len(cuts) > 0:
        result = steps_of(own_key, extent, cuts, -0.22, 0.18) * result
    return jnp.clip(result, min=-bound, max=bound).astype(held_as)


def setup_inputs(seed: int = 0) -> dict:
    key_list = jax.random.split(jax.random.key(seed), 7)
    query = draw_query(jax.random.fold_in(key_list[6], 71), 0)
    grad_out = gaussian(key_list[1], (TILES, TILE, H * DH), 1.0, 6.0, ((0, 256),))
    branch_kv = gaussian(key_list[2], (TILES, TILE, 2 * KVH * DH), 1.0, 6.0, ((0, 256),))
    root_kv = draw_root_kv(jax.random.fold_in(key_list[6], 71), 0)
    lengths = draw_lengths(jax.random.fold_in(key_list[6], 71), 0)
    segments = place_ends(jax.random.randint(key_list[5], (TILES,), 0, SEGS), jax.random.fold_in(key_list[5], 1), 0, SEGS - 1).astype(jnp.int32)
    return dict(query=query, grad_out=grad_out, branch_kv=branch_kv, root_kv=root_kv, lengths=lengths, segments=segments)


def tile_grads(query, grad, branch, length, segment, root_keys):
    rows = query.shape[0]
    width = KVH * DH
    groups = H // KVH
    roots = root_keys.shape[0]
    everything = jnp.concatenate([root_keys, branch], axis=0)
    span = roots + rows
    scale = DH ** -0.5
    row_pos = lax.broadcasted_iota(jnp.int32, (rows, span), 0)
    col_pos = lax.broadcasted_iota(jnp.int32, (rows, span), 1)
    visible = jnp.where(col_pos < roots, col_pos < (segment + 1) * (roots // SEGS), col_pos - roots <= row_pos)
    live = lax.broadcasted_iota(jnp.int32, (rows, 1), 0) < length
    grad = jnp.where(live, grad, jnp.zeros_like(grad))
    dq_parts = []
    dk_parts = []
    dv_parts = []
    for head in range(KVH):
        q_head = query[:, head * groups * DH:(head + 1) * groups * DH].reshape(rows, groups, DH).astype(jnp.float32)
        g_head = grad[:, head * groups * DH:(head + 1) * groups * DH].reshape(rows, groups, DH).astype(jnp.float32)
        k_head = everything[:, head * DH:(head + 1) * DH].astype(jnp.float32)
        v_head = everything[:, width + head * DH:width + (head + 1) * DH].astype(jnp.float32)
        scores = jnp.einsum('tgd,ld->gtl', q_head, k_head) * scale
        scores = jnp.where(visible[None], scores, jnp.float32(-1e30))
        peak = jnp.max(scores, axis=-1, keepdims=True)
        weights = jnp.exp(scores - peak)
        weights = weights / jnp.sum(weights, axis=-1, keepdims=True)
        probs = weights.astype(jnp.bfloat16).astype(jnp.float32)
        output = jnp.einsum('gtl,ld->tgd', probs, v_head)
        delta = jnp.sum(g_head * output, axis=-1)
        dv_parts.append(jnp.einsum('gtl,tgd->ld', probs, g_head))
        prob_grad = jnp.einsum('tgd,ld->gtl', g_head, v_head)
        score_grad = (weights * (prob_grad - delta.T[:, :, None]) * scale).astype(jnp.bfloat16).astype(jnp.float32)
        dq_parts.append(jnp.einsum('gtl,ld->tgd', score_grad, k_head).reshape(rows, groups * DH))
        dk_parts.append(jnp.einsum('gtl,tgd->ld', score_grad, q_head))
    dq = jnp.concatenate(dq_parts, axis=1).astype(jnp.bfloat16)
    dkv = jnp.concatenate(dk_parts + dv_parts, axis=1)
    return dq, dkv[roots:].astype(jnp.bfloat16), dkv[:roots]


def reference(query, grad_out, branch_kv, root_kv, lengths, segments):
    def step(total, items):
        q_tile, g_tile, b_tile, length, segment = items

        def work():
            return tile_grads(q_tile, g_tile, b_tile, length, segment, root_kv)

        def skip():
            return (jnp.zeros(q_tile.shape, jnp.bfloat16), jnp.zeros(b_tile.shape, jnp.bfloat16), jnp.zeros(root_kv.shape, jnp.float32))

        dq, dbranch, droot = lax.cond(length > 0, work, skip)
        return total + droot, (dq, dbranch)

    total, (query_grad, branch_grad) = lax.scan(step, jnp.zeros(root_kv.shape, jnp.float32), (query, grad_out, branch_kv, lengths, segments))
    return query_grad, branch_grad, total
```

```python
import functools
import math

import jax
import jax.numpy as jnp
from jax import lax
from jax.experimental import pallas as pl
from jax.experimental.pallas import tpu as pltpu
from jax.sharding import PartitionSpec as P

KVH = 4
GROUP = 8
DH = 128
TILE = 128
R = 1024
SEGS = 4
NX, NY, NZ = 4, 4, 8
CHUNKS = 2 * KVH
WIDTH = KVH * DH
SCALE = DH**-0.5
SCALE_LOG2 = SCALE * math.log2(math.e)
PACK = 4

F32 = jnp.float32
BF16 = jnp.bfloat16
MESH = pl.DeviceIdType.MESH
NT = (((1,), (1,)), ((), ()))
NN = (((1,), (0,)), ((), ()))


def dot(a, b, dims):
    return lax.dot_general(a, b, dims, preferred_element_type=F32)


def softmax_grads(q, g, segment, keys, values, branch_keys, branch_values, p_ref, ds_ref):
    rows = PACK * TILE
    row_pos = lax.rem(lax.broadcasted_iota(jnp.int32, (rows, TILE), 0), TILE)
    col_pos = lax.broadcasted_iota(jnp.int32, (rows, TILE), 1)
    part = R // SEGS
    s_root = [dot(q, keys[b * part : (b + 1) * part], NT) for b in range(SEGS)]
    s_branch = jnp.where(col_pos <= row_pos, dot(q, branch_keys, NT), F32(-1e30))
    peak = jnp.maximum(
        jnp.max(s_branch, axis=1, keepdims=True), jnp.max(s_root[0], axis=1, keepdims=True)
    )
    for b in range(1, SEGS):
        of_part = jnp.max(s_root[b], axis=1, keepdims=True)
        peak = jnp.maximum(peak, jnp.where(b <= segment, of_part, F32(-1e30)))
    shift = peak * SCALE_LOG2
    w_branch = jnp.exp2(s_branch * SCALE_LOG2 - shift)
    total = jnp.sum(w_branch, axis=1, keepdims=True)
    w_root = []
    for b in range(SEGS):
        own_shift = shift if b == 0 else jnp.where(b <= segment, shift, F32(1e30))
        w = jnp.exp2(s_root[b] * SCALE_LOG2 - own_shift)
        total = total + jnp.sum(w, axis=1, keepdims=True)
        w_root.append(w)
    inverse = 1.0 / total
    w_branch = w_branch * inverse
    w_root = [w * inverse for w in w_root]
    d_branch = dot(g, branch_values, NT)
    d_root = [dot(g, values[b * part : (b + 1) * part], NT) for b in range(SEGS)]
    delta = jnp.sum(w_branch * d_branch, axis=1, keepdims=True)
    for b in range(SEGS):
        delta = delta + jnp.sum(w_root[b] * d_root[b], axis=1, keepdims=True)
    for b in range(SEGS):
        p_ref[:, b * part : (b + 1) * part] = w_root[b].astype(BF16)
        ds_ref[:, b * part : (b + 1) * part] = (w_root[b] * (d_root[b] - delta)).astype(BF16)
    p_ref[:, R:] = w_branch.astype(BF16)
    ds_ref[:, R:] = (w_branch * (d_branch - delta)).astype(BF16)


def kernel(
    lengths,
    segments,
    q_hbm,
    g_hbm,
    branch_hbm,
    root_ref,
    dq_hbm,
    db_hbm,
    out_ref,
    q_s,
    g_s,
    branch_s,
    kv,
    dq_s,
    db_s,
    p_s,
    ds_s,
    dk_acc,
    dv_acc,
    dpart,
    r0,
    s1,
    r1,
    s2,
    r2,
    in_sem,
    out_sem,
    z_send,
    z_recv,
    y_send,
    y_recv,
    c_send,
    c_recv,
    s0_send,
    s0_recv,
    s1_send,
    s1_recv,
    s2_send,
    s2_recv,
):
    grp = lax.axis_index("grp")
    dev = lax.axis_index("dev")
    x, z_lo = grp // 2, grp % 2
    y, z_hi, c = dev // 8, (dev // 2) % 4, dev % 2
    z = 2 * z_hi + z_lo

    def at(px, py, pz, pc):
        return (px * 2 + pz % 2, py * 8 + (pz // 2) * 2 + pc)

    def ring_z(offset):
        return (z + offset + NZ) % NZ

    away = 2 * z_lo - 1
    z_dests = [at(x, y, ring_z(away * k), c) for k in (1, 2, 3)]
    z_sources = [at(x, y, ring_z(away * k), c) for k in (1, 3, -2)]
    y_dests = [at(x, (y + k) % NY, z, c) for k in (1, 2, 3)]
    other_core = at(x, y, z, 1 - c)
    plane = [((x + k // NY) % NX, (y + k % NY) % NY) for k in range(1, NX * NY)]
    final_dests = [((x + k // 2) % NX, 2 * x + k % 2) for k in range(2 * NX)]

    q_copies = [pltpu.make_async_copy(q_hbm.at[t], q_s.at[t], in_sem.at[t]) for t in range(2)]
    g_copies = [pltpu.make_async_copy(g_hbm.at[t], g_s.at[t], in_sem.at[2 + t]) for t in range(2)]
    b_copy = pltpu.make_async_copy(branch_hbm, branch_s, in_sem.at[4])
    for copy in (b_copy, q_copies[0], g_copies[0], q_copies[1], g_copies[1]):
        copy.start()

    barrier = pltpu.get_barrier_semaphore()

    def greet(device):
        pl.semaphore_signal(barrier, inc=1, device_id=device, device_id_type=MESH)

    greet(other_core)
    for px, py in plane:
        greet(at(px, py, z, c))
    for device in z_dests + z_sources:
        greet(device)
    for px, pz in final_dests:
        own = jnp.logical_and(px == x, pz == z)
        pl.when(jnp.logical_not(own))(functools.partial(greet, at(px, y, pz, c)))
    for k in range(NZ):
        pz = (z + k) % NZ
        own = jnp.logical_and(z_hi == x, pz == z)
        pl.when(jnp.logical_not(own))(functools.partial(greet, at(z_hi, y, pz, c)))
    own_final = jnp.where(z_hi == x, 2, 0)
    pl.semaphore_wait(barrier, 1 + 15 + 6 + 16 - own_final)

    def remote(src, dst, send_sem, recv_sem, device):
        return pltpu.make_async_remote_copy(
            src_ref=src,
            dst_ref=dst,
            send_sem=send_sem,
            recv_sem=recv_sem,
            device_id=device,
            device_id_type=MESH,
        )

    def arrived(ref, sem):
        pltpu.make_async_copy(ref, ref, sem).wait()

    def gather_z(chunk):
        start = (chunk % 2) * WIDTH + (chunk // 2) * DH
        src = root_ref.at[:, start : start + DH]
        dst = kv.at[chunk, y, c, z_hi]
        pltpu.make_async_copy(src, dst, z_recv.at[chunk]).start()
        for device in z_dests:
            remote(src, dst, z_send, z_recv.at[chunk], device).start()

    def gather_y(chunk):
        block = kv.at[chunk, y, c]
        arrived(block, z_recv.at[chunk])
        for device in y_dests:
            remote(block, block, y_send, y_recv.at[chunk], device).start()

    def gather_core(chunk):
        arrived(kv.at[chunk, pl.ds(0, 3), c], y_recv.at[chunk])
        block = kv.at[chunk, :, c]
        remote(block, block, c_send, c_recv.at[chunk], other_core).start()

    def gathered(chunk):
        arrived(kv.at[chunk, :, 1 - c], c_recv.at[chunk])

    def reduce_core(chunk):
        remote(dpart.at[chunk, :, 1 - c], r0.at[chunk], s0_send, s0_recv.at[chunk], other_core).start()

    def reduce_plane(chunk):
        arrived(r0.at[chunk], s0_recv.at[chunk])
        s1[chunk] = (dpart[chunk, :, c].astype(F32) + r0[chunk].astype(F32)).astype(BF16)
        for k, (px, py) in enumerate(plane):
            remote(
                s1.at[chunk, py, px], r1.at[chunk, k], s1_send, s1_recv.at[chunk], at(px, py, z, c)
            ).start()

    def reduce_groups(chunk):
        arrived(r1.at[chunk], s1_recv.at[chunk])
        s2[chunk] = (s1[chunk, y, x].astype(F32) + jnp.sum(r1[chunk].astype(F32), axis=0)).astype(BF16)
        for px, pz in final_dests:
            own = jnp.logical_and(px == x, pz == z)

            @pl.when(own)
            def _():
                pltpu.make_async_copy(s2.at[chunk], r2.at[chunk, z], s2_recv.at[chunk]).start()

            @pl.when(jnp.logical_not(own))
            def _():
                remote(s2.at[chunk], r2.at[chunk, z], s2_send, s2_recv.at[chunk], at(px, y, pz, c)).start()

    def reduce_done(chunk):
        arrived(r2.at[chunk], s2_recv.at[chunk])
        start = pl.multiple_of((chunk % 2) * WIDTH + (chunk // 2) * DH, DH)
        out_ref[:, pl.ds(start, DH)] = jnp.sum(r2[chunk].astype(F32), axis=0)

    for chunk in range(CHUNKS):
        gather_z(chunk)
    gather_y(0)
    gather_y(1)
    gather_core(0)
    gather_core(1)
    b_copy.wait()
    gathered(0)
    gathered(1)

    def both(stage, head):
        stage(2 * head + 1)
        stage(2 * head)

    def step(index, carry):
        head, t = index // 2, index % 2

        @pl.when(index == 0)
        def _():
            q_copies[0].wait()
            g_copies[0].wait()

        @pl.when(index == 1)
        def _():
            q_copies[1].wait()
            g_copies[1].wait()

        @pl.when(jnp.logical_and(t == 0, head > 0))
        def _():
            gathered(2 * head)
            gathered(2 * head + 1)

        @pl.when(jnp.logical_and(t == 0, head < KVH - 1))
        def _():
            gather_y(2 * head + 2)
            gather_y(2 * head + 3)

        @pl.when(jnp.logical_and(t == 1, head < KVH - 1))
        def _():
            gather_core(2 * head + 2)
            gather_core(2 * head + 3)

        length, segment = lengths[t], segments[t]
        live = lax.broadcasted_iota(jnp.int32, (TILE, DH), 0) < length
        keys = kv[2 * head].reshape(R, DH)
        values = kv[2 * head + 1].reshape(R, DH)
        k_cols = pl.ds(pl.multiple_of(head * DH, DH), DH)
        v_cols = pl.ds(pl.multiple_of(WIDTH + head * DH, DH), DH)
        branch_keys = branch_s[t, :, k_cols]
        branch_values = branch_s[t, :, v_cols]
        q_t, g_t = [], []
        for first in range(0, GROUP, PACK):
            qs, gs = [], []
            for j in range(first, first + PACK):
                cols = pl.ds(pl.multiple_of((head * GROUP + j) * DH, DH), DH)
                qs.append(q_s[t, :, cols])
                gs.append(jnp.where(live, g_s[t, :, cols], jnp.zeros((), BF16)))
            rows = pl.ds(first * TILE, PACK * TILE)
            softmax_grads(
                jnp.concatenate(qs, axis=0),
                jnp.concatenate(gs, axis=0),
                segment,
                keys,
                values,
                branch_keys,
                branch_values,
                p_s.at[rows],
                ds_s.at[rows],
            )
            dq = dot(ds_s[rows, :R], keys, NN) + dot(ds_s[rows, R:], branch_keys, NN)
            dq = (dq * SCALE).astype(BF16)
            for j in range(PACK):
                cols = pl.ds(pl.multiple_of((head * GROUP + first + j) * DH, DH), DH)
                dq_s[t, :, cols] = dq[j * TILE : (j + 1) * TILE]
            q_t += [block.T for block in qs]
            g_t += [block.T for block in gs]
        dk = dot(jnp.concatenate(q_t, axis=1), ds_s[...], NN) * SCALE
        dv = dot(jnp.concatenate(g_t, axis=1), p_s[...], NN)
        db_s[t, :, k_cols] = dk[:, R:].T.astype(BF16)
        db_s[t, :, v_cols] = dv[:, R:].T.astype(BF16)
        heads = pl.ds(pl.multiple_of(head * GROUP * DH, GROUP * DH), GROUP * DH)
        pltpu.make_async_copy(dq_s.at[t, :, heads], dq_hbm.at[t, :, heads], out_sem.at[0]).start()

        @pl.when(t == 0)
        def _():
            dk_acc[...] = dk[:, :R]
            dv_acc[...] = dv[:, :R]

        @pl.when(t == 1)
        def _():
            shape = (NY, 2, NZ // 2, R // 32, DH)
            dpart[2 * head + 1] = (dv_acc[...] + dv[:, :R]).T.astype(BF16).reshape(shape)
            reduce_core(2 * head + 1)
            dpart[2 * head] = (dk_acc[...] + dk[:, :R]).T.astype(BF16).reshape(shape)
            reduce_core(2 * head)

        @pl.when(jnp.logical_and(t == 0, head >= 2))
        def _():
            both(reduce_done, head - 2)

        @pl.when(jnp.logical_and(t == 0, head >= 1))
        def _():
            both(reduce_plane, head - 1)

        @pl.when(jnp.logical_and(t == 1, head >= 1))
        def _():
            both(reduce_groups, head - 1)

        return carry

    lax.fori_loop(0, 2 * KVH, step, 0)
    db_copy = pltpu.make_async_copy(db_s, db_hbm, out_sem.at[1])
    db_copy.start()
    both(reduce_plane, KVH - 1)
    both(reduce_done, KVH - 2)
    both(reduce_groups, KVH - 1)
    both(reduce_done, KVH - 1)

    arrived(dq_s, out_sem.at[0])
    db_copy.wait()
    for _ in range(3):
        arrived(kv.at[:, 0, 0, 0], z_send)
        arrived(kv.at[:, 0, 0], y_send)
    arrived(kv.at[:, :, 0], c_send)
    arrived(r0, s0_send)
    arrived(r1, s1_send)

    @pl.when(z_hi == x)
    def _():
        arrived(r2.at[:, pl.ds(0, 7)], s2_send)

    @pl.when(z_hi != x)
    def _():
        arrived(r2, s2_send)


def local(query, grad_out, branch_kv, root_kv, lengths, segments):
    rows = R // 32
    anywhere = pl.BlockSpec(memory_space=pl.ANY)
    vmem = pl.BlockSpec(memory_space=pltpu.VMEM)
    smem = pl.BlockSpec(memory_space=pltpu.SMEM)
    dma = pltpu.SemaphoreType.DMA
    blocks = (CHUNKS, NY, 2, NZ // 2, rows, DH)
    half = (CHUNKS, NY, NZ // 2, rows, DH)
    return pl.pallas_call(
        kernel,
        out_shape=(
            jax.ShapeDtypeStruct(query.shape, BF16),
            jax.ShapeDtypeStruct(branch_kv.shape, BF16),
            jax.ShapeDtypeStruct(root_kv.shape, F32),
        ),
        in_specs=[smem, smem, anywhere, anywhere, anywhere, vmem],
        out_specs=(anywhere, anywhere, vmem),
        scratch_shapes=[
            pltpu.VMEM(query.shape, BF16),
            pltpu.VMEM(query.shape, BF16),
            pltpu.VMEM(branch_kv.shape, BF16),
            pltpu.VMEM(blocks, BF16),
            pltpu.VMEM(query.shape, BF16),
            pltpu.VMEM(branch_kv.shape, BF16),
            pltpu.VMEM((GROUP * TILE, R + TILE), BF16),
            pltpu.VMEM((GROUP * TILE, R + TILE), BF16),
            pltpu.VMEM((DH, R), F32),
            pltpu.VMEM((DH, R), F32),
            pltpu.VMEM(blocks, BF16),
            pltpu.VMEM(half, BF16),
            pltpu.VMEM(half, BF16),
            pltpu.VMEM((CHUNKS, NX * NY - 1, rows, DH), BF16),
            pltpu.VMEM((CHUNKS, rows, DH), BF16),
            pltpu.VMEM((CHUNKS, NZ, rows, DH), BF16),
            dma((5,)),
            dma((2,)),
            dma,
            dma((CHUNKS,)),
            dma,
            dma((CHUNKS,)),
            dma,
            dma((CHUNKS,)),
            dma,
            dma((CHUNKS,)),
            dma,
            dma((CHUNKS,)),
            dma,
            dma((CHUNKS,)),
        ],
        compiler_params=pltpu.CompilerParams(
            collective_id=0, has_side_effects=True, vmem_limit_bytes=60 << 20
        ),
    )(lengths, segments, query, grad_out, branch_kv, root_kv)


def solution(mesh):
    placed = (
        P(("grp", "dev"), None, None),
        P(("grp", "dev"), None, None),
        P(("grp", "dev"), None, None),
        P("dev", None),
        P(("grp", "dev")),
        P(("grp", "dev")),
    )
    return jax.shard_map(
        local,
        mesh=mesh,
        in_specs=placed,
        out_specs=(P(("grp", "dev"), None, None), P(("grp", "dev"), None, None), P("dev", None)),
        check_vma=False,
    )
```

```python
import functools
import math

import jax
import jax.numpy as jnp
from jax import lax
from jax.experimental import pallas as pl
from jax.experimental.pallas import tpu as pltpu
from jax.sharding import PartitionSpec as P

KVH = 4
GROUP = 8
DH = 128
TILE = 128
R = 1024
SEGS = 4
NX, NY, NZ = 4, 4, 8
CHUNKS = 2 * KVH
WIDTH = KVH * DH
SCALE = DH**-0.5
SCALE_LOG2 = SCALE * math.log2(math.e)
PACK = 4
ROWS = 16
AHEAD = 3

F32 = jnp.float32
BF16 = jnp.bfloat16
MESH = pl.DeviceIdType.MESH
NT = (((1,), (1,)), ((), ()))
NN = (((1,), (0,)), ((), ()))


def dot(a, b, dims):
    return lax.dot_general(a, b, dims, preferred_element_type=F32)


TILES = R // DH + 1
OF_PART = R // SEGS // DH


def tile_of(ref, first, b):
    return ref[pl.ds(first, ROWS), b * DH : (b + 1) * DH]


def across(x, reduce):
    return jnp.broadcast_to(reduce(x, axis=1, keepdims=True), (ROWS, DH))


def peaks(first, segment, s_ref, stats):
    row_pos = first % TILE + lax.broadcasted_iota(jnp.int32, (ROWS, DH), 0)
    col_pos = lax.broadcasted_iota(jnp.int32, (ROWS, DH), 1)
    branch = jnp.where(col_pos <= row_pos, tile_of(s_ref, first, TILES - 1), F32(-1e30))
    peak = branch
    for part in range(SEGS):
        top = tile_of(s_ref, first, part * OF_PART)
        for b in range(part * OF_PART + 1, (part + 1) * OF_PART):
            top = jnp.maximum(top, tile_of(s_ref, first, b))
        seen = top if part == 0 else jnp.where(part <= segment, top, F32(-1e30))
        peak = jnp.maximum(peak, seen)
    stats[0, pl.ds(first, ROWS)] = across(peak, jnp.max) * SCALE_LOG2


def exponentials(first, segment, s_ref, d_ref, stats):
    rows = pl.ds(first, ROWS)
    row_pos = first % TILE + lax.broadcasted_iota(jnp.int32, (ROWS, DH), 0)
    col_pos = lax.broadcasted_iota(jnp.int32, (ROWS, DH), 1)
    shift = stats[0, rows]
    total = delta = None
    for b in range(TILES):
        score = tile_of(s_ref, first, b)
        own_shift = shift
        if b == TILES - 1:
            own_shift = jnp.where(col_pos <= row_pos, shift, F32(1e30))
        elif b >= OF_PART:
            own_shift = jnp.where(b // OF_PART <= segment, shift, F32(1e30))
        e = jnp.exp2(score * SCALE_LOG2 - own_shift)
        s_ref[rows, b * DH : (b + 1) * DH] = e
        term = e * tile_of(d_ref, first, b)
        total = e if total is None else total + e
        delta = term if delta is None else delta + term
    inverse = 1.0 / across(total, jnp.sum)
    stats[1, rows] = inverse
    stats[2, rows] = across(delta, jnp.sum) * inverse


def weigh(first, s_ref, d_ref, p_ref, ds_ref, stats):
    rows = pl.ds(first, ROWS)
    inverse, delta = stats[1, rows], stats[2, rows]
    for b in range(TILES):
        cols = slice(b * DH, (b + 1) * DH)
        w = tile_of(s_ref, first, b) * inverse
        p_ref[rows, cols] = w.astype(BF16)
        ds_ref[rows, cols] = (w * (tile_of(d_ref, first, b) - delta)).astype(BF16)


def interleaved(many, few):
    done = 0
    for i, piece in enumerate(many):
        piece()
        while done < len(few) and (done + 1) * len(many) <= (i + 1) * len(few):
            few[done]()
            done += 1
    assert done == len(few)


def kernel(
    lengths,
    segments,
    q_hbm,
    g_hbm,
    branch_hbm,
    root_ref,
    dq_ref,
    db_ref,
    out_ref,
    q_s,
    g_s,
    branch_s,
    kv,
    sa,
    sb,
    da,
    db,
    pa,
    pb,
    ds_a,
    ds_b,
    q_t,
    g_t,
    acc,
    branch_acc,
    stats,
    dpart,
    r0,
    s1,
    r1,
    s2,
    r2,
    s3,
    r3,
    in_sem,
    z_send,
    z_recv,
    y_send,
    y_recv,
    c_send,
    c_recv,
    s0_send,
    s0_recv,
    s1_send,
    s1_recv,
    s2_send,
    s2_recv,
    s3_send,
    s3_recv,
):
    grp = lax.axis_index("grp")
    dev = lax.axis_index("dev")
    x, z_lo = grp // 2, grp % 2
    y, z_hi, c = dev // 8, (dev // 2) % 4, dev % 2
    z = 2 * z_hi + z_lo

    def at(px, py, pz, pc):
        return (px * 2 + pz % 2, py * 8 + (pz // 2) * 2 + pc)

    def ring_z(offset):
        return (z + offset + NZ) % NZ

    away = 2 * z_lo - 1
    z_dests = [at(x, y, ring_z(away * k), c) for k in (1, 2, 3)]
    y_dests = [at(x, (y + k) % NY, z, c) for k in (1, 2, 3)]
    other_core = at(x, y, z, 1 - c)
    plane = [((x + k // NY) % NX, (y + k % NY) % NY) for k in range(1, NX * NY)]
    column = [(z + k) % NZ for k in range(1, NZ)]
    x_dests = [at((x + k) % NX, y, z, c) for k in (1, 2, 3)]

    q_copies = [pltpu.make_async_copy(q_hbm.at[t], q_s.at[t], in_sem.at[t]) for t in range(2)]
    g_copies = [pltpu.make_async_copy(g_hbm.at[t], g_s.at[t], in_sem.at[2 + t]) for t in range(2)]
    b_copy = pltpu.make_async_copy(branch_hbm, branch_s, in_sem.at[4])
    for copy in (b_copy, q_copies[0], g_copies[0], q_copies[1], g_copies[1]):
        copy.start()

    barrier = pltpu.get_barrier_semaphore()

    def greet(device):
        pl.semaphore_signal(barrier, inc=1, device_id=device, device_id_type=MESH)

    greet(other_core)
    for px, py in plane:
        greet(at(px, py, z, c))
    for pz in column:
        greet(at(x, y, pz, c))
    pl.semaphore_wait(barrier, 1 + len(plane) + len(column))

    def remote(src, dst, send_sem, recv_sem, device):
        return pltpu.make_async_remote_copy(
            src_ref=src,
            dst_ref=dst,
            send_sem=send_sem,
            recv_sem=recv_sem,
            device_id=device,
            device_id_type=MESH,
        )

    def arrived(ref, sem):
        pltpu.make_async_copy(ref, ref, sem).wait()

    def gather_z(chunk):
        start = (chunk % 2) * WIDTH + (chunk // 2) * DH
        src = root_ref.at[:, start : start + DH]
        dst = kv.at[chunk, y, c, z_hi]
        pltpu.make_async_copy(src, dst, z_recv.at[chunk]).start()
        for device in z_dests:
            remote(src, dst, z_send, z_recv.at[chunk], device).start()

    def gather_y(chunk):
        block = kv.at[chunk, y, c]
        arrived(block, z_recv.at[chunk])
        for device in y_dests:
            remote(block, block, y_send, y_recv.at[chunk], device).start()

    def gather_core(chunk):
        arrived(kv.at[chunk, pl.ds(0, 3), c], y_recv.at[chunk])
        block = kv.at[chunk, :, c]
        remote(block, block, c_send, c_recv.at[chunk], other_core).start()

    def gathered(chunk):
        arrived(kv.at[chunk, :, 1 - c], c_recv.at[chunk])

    def reduce_core(head):
        remote(dpart.at[head, :, 1 - c], r0.at[head], s0_send, s0_recv.at[head], other_core).start()

    def reduce_plane(head):
        arrived(r0.at[head], s0_recv.at[head])
        s1[head] = (dpart[head, :, c].astype(F32) + r0[head].astype(F32)).astype(BF16)
        for k, (px, py) in enumerate(plane):
            remote(
                s1.at[head, py, px], r1.at[head, k], s1_send, s1_recv.at[head], at(px, py, z, c)
            ).start()

    def reduce_column(head):
        arrived(r1.at[head], s1_recv.at[head])
        s2[head] = (s1[head, y, x].astype(F32) + jnp.sum(r1[head].astype(F32), axis=0)).astype(BF16)
        for k, pz in enumerate(column):
            remote(
                s2.at[head, pz // 2], r2.at[head, k], s2_send, s2_recv.at[head], at(x, y, pz, c)
            ).start()

    def share_sum(head):
        arrived(r2.at[head], s2_recv.at[head])
        summed = s2[head, z_hi].astype(F32) + jnp.sum(r2[head].astype(F32), axis=0)
        s3[head] = summed
        r3[head, x] = summed
        for device in x_dests:
            remote(s3.at[head], r3.at[head, x], s3_send, s3_recv.at[head], device).start()

    def reduce_done(head):
        arrived(r3.at[head, pl.ds(0, 3)], s3_recv.at[head])
        for part in range(NX):
            cols = pl.ds(pl.multiple_of((part // 2) * WIDTH + head * DH, DH), DH)
            out_ref[(part % 2) * 16 : (part % 2 + 1) * 16, cols] = r3[head, part]

    ds_s = (ds_a, ds_b)

    def columns(first, count=1):
        return pl.ds(pl.multiple_of(first * DH, DH), count * DH)

    def scores_of(index, pack, s_ref, d_ref):
        head, t = index // 2, index % 2
        live = lax.broadcasted_iota(jnp.int32, (TILE, DH), 0) < lengths[t]
        first = head * GROUP + pack * PACK
        qs = [q_s[t, :, columns(first + j)] for j in range(PACK)]
        gs = [
            jnp.where(live, g_s[t, :, columns(first + j)], jnp.zeros((), BF16)) for j in range(PACK)
        ]
        q, g = jnp.concatenate(qs, axis=0), jnp.concatenate(gs, axis=0)

        def turn():
            for j in range(PACK):
                q_t[pack, :, j * TILE : (j + 1) * TILE] = qs[j].T
                g_t[pack, :, j * TILE : (j + 1) * TILE] = gs[j].T

        def root(of, ref, chunk, b):
            part = kv[chunk, b].reshape(R // SEGS, DH)
            ref[:, b * R // SEGS : (b + 1) * R // SEGS] = dot(of, part, NT)

        def branch(of, ref, start):
            ref[:, R:] = dot(of, branch_s[t, :, columns(start + head)], NT)

        pieces = []
        for of, ref, kind in ((q, s_ref, 0), (g, d_ref, 1)):
            pieces += [functools.partial(root, of, ref, 2 * head + kind, b) for b in range(SEGS)]
            pieces.append(functools.partial(branch, of, ref, kind * KVH))
        return pieces + [turn]

    def key_grads(index, pack, p_ref, is_first):
        part = R // SEGS

        def root(kind, ref, rows_t, b):
            cols = slice(b * part, (b + 1) * part)
            acc[kind, :, cols] = acc[kind, :, cols] + dot(rows_t[pack], ref[:, cols], NN)

        def branch(kind, ref, rows_t):
            term = dot(rows_t[pack], ref[:, R:], NN)
            branch_acc[kind] = term if is_first else branch_acc[kind] + term

        pieces = []
        for kind, ref, rows_t in ((1, p_ref, g_t), (0, ds_s[pack].at[index], q_t)):
            pieces += [functools.partial(root, kind, ref, rows_t, b) for b in range(SEGS)]
            pieces.append(functools.partial(branch, kind, ref, rows_t))
        return pieces

    def softmax_of(index, pack, s_ref, d_ref, p_ref):
        segment = segments[index % 2]
        ds_ref = ds_s[pack].at[index]
        count = PACK * TILE // ROWS

        def piece(i):
            if i + 2 * AHEAD < count:
                peaks((i + 2 * AHEAD) * ROWS, segment, s_ref, stats)
            if 0 <= i + AHEAD < count:
                exponentials((i + AHEAD) * ROWS, segment, s_ref, d_ref, stats)
            if i >= 0:
                weigh(i * ROWS, s_ref, d_ref, p_ref, ds_ref, stats)

        return [functools.partial(piece, i) for i in range(-2 * AHEAD, count)]

    def put_branch(index):
        head, t = index // 2, index % 2
        db_ref[t, :, columns(head)] = (branch_acc[0].T * SCALE).astype(BF16)
        db_ref[t, :, columns(KVH + head)] = branch_acc[1].T.astype(BF16)

    def put_root(head):
        shape = (NY, 2, NZ // 2, 2, 16, DH)
        for kind in range(2):
            rows = acc[kind].T
            rows = (rows * SCALE if kind == 0 else rows).astype(BF16).reshape(shape)
            for half in range(2):
                dpart[head, :, :, 2 * kind + half] = rows[:, :, :, half]
        acc[...] = jnp.zeros_like(acc)
        reduce_core(head)

    for chunk in range(CHUNKS):
        gather_z(chunk)
    for chunk in range(2):
        gather_y(chunk)
    acc[...] = jnp.zeros_like(acc)
    branch_acc[...] = jnp.zeros_like(branch_acc)
    q_t[1] = jnp.zeros_like(q_t[1])
    g_t[1] = jnp.zeros_like(g_t[1])
    pb[...] = jnp.zeros_like(pb)
    ds_b[2 * KVH] = jnp.zeros_like(pb)
    for chunk in range(2):
        gather_core(chunk)
    for chunk in range(2, 4):
        gather_y(chunk)
    b_copy.wait()
    q_copies[0].wait()
    g_copies[0].wait()
    gathered(0)
    gathered(1)
    for piece in scores_of(0, 0, sa, da):
        piece()

    def step(index, carry):
        head, t = index // 2, index % 2
        before = jnp.where(index == 0, 2 * KVH, index - 1)
        after = jnp.minimum(index + 1, 2 * KVH - 1)

        @pl.when(index == 0)
        def _():
            q_copies[1].wait()
            g_copies[1].wait()
            for chunk in range(4, CHUNKS):
                gather_y(chunk)

        interleaved(
            softmax_of(index, 0, sa, da, pa),
            key_grads(before, 1, pb, False) + scores_of(index, 1, sb, db),
        )

        @pl.when(index > 0)
        def _():
            put_branch(before)

        @pl.when(jnp.logical_and(t == 0, head >= 1))
        def _():
            put_root(head - 1)

        @pl.when(jnp.logical_and(t == 0, head < KVH - 1))
        def _():
            gather_core(2 * head + 2)
            gather_core(2 * head + 3)

        @pl.when(jnp.logical_and(t == 1, head < KVH - 1))
        def _():
            gathered(2 * head + 2)
            gathered(2 * head + 3)

        @pl.when(jnp.logical_and(t == 1, head >= 1))
        def _():
            reduce_plane(head - 1)

        @pl.when(jnp.logical_and(t == 1, head >= 2))
        def _():
            reduce_column(head - 2)

        interleaved(
            softmax_of(index, 1, sb, db, pb),
            key_grads(index, 0, pa, True) + scores_of(after, 0, sa, da),
        )

        @pl.when(jnp.logical_and(t == 0, head == KVH - 1))
        def _():
            share_sum(head - 3)

        return carry

    def query_grads(index, carry):
        head, t = index // 2, index % 2
        k_cols = pl.ds(pl.multiple_of(head * DH, DH), DH)
        for pack in range(2):
            rows = ds_s[pack].at[index]
            dq = dot(rows[:, :R], kv[2 * head].reshape(R, DH), NN)
            dq = dq + dot(rows[:, R:], branch_s[t, :, k_cols], NN)
            dq = (dq * SCALE).astype(BF16)
            for j in range(PACK):
                cols = columns(head * GROUP + pack * PACK + j)
                dq_ref[t, :, cols] = dq[j * TILE : (j + 1) * TILE]
        return carry

    last = KVH - 1
    lax.fori_loop(0, 2 * KVH, step, 0)
    for piece in key_grads(2 * KVH - 1, 1, pb, False):
        piece()
    put_root(last)
    put_branch(2 * KVH - 1)
    reduce_column(last - 1)
    lax.fori_loop(0, 1, query_grads, 0)
    reduce_plane(last)
    share_sum(last - 2)
    reduce_done(last - 3)
    lax.fori_loop(1, 5, query_grads, 0)
    share_sum(last - 1)
    reduce_column(last)
    reduce_done(last - 2)
    lax.fori_loop(5, 8, query_grads, 0)
    reduce_done(last - 1)
    share_sum(last)
    reduce_done(last)

    for _ in range(3):
        arrived(kv.at[:, 0, 0, 0], z_send)
        arrived(kv.at[:, 0, 0], y_send)
    arrived(kv.at[:, :, 0], c_send)
    arrived(r0, s0_send)
    arrived(r1, s1_send)
    arrived(r2, s2_send)
    arrived(r3.at[:, pl.ds(0, 3)], s3_send)


def local(query, grad_out, branch_kv, root_kv, lengths, segments):
    rows = R // 32
    anywhere = pl.BlockSpec(memory_space=pl.ANY)
    vmem = pl.BlockSpec(memory_space=pltpu.VMEM)
    smem = pl.BlockSpec(memory_space=pltpu.SMEM)
    dma = pltpu.SemaphoreType.DMA
    blocks = (CHUNKS, NY, 2, NZ // 2, rows, DH)
    half = (KVH, NY, NX, NZ // 2, 16, DH)
    return pl.pallas_call(
        kernel,
        out_shape=(
            jax.ShapeDtypeStruct(query.shape, BF16),
            jax.ShapeDtypeStruct(branch_kv.shape, BF16),
            jax.ShapeDtypeStruct(root_kv.shape, F32),
        ),
        in_specs=[smem, smem, anywhere, anywhere, anywhere, vmem],
        out_specs=(vmem, vmem, vmem),
        scratch_shapes=[
            pltpu.VMEM(query.shape, BF16),
            pltpu.VMEM(query.shape, BF16),
            pltpu.VMEM(branch_kv.shape, BF16),
            pltpu.VMEM(blocks, BF16),
            *[pltpu.VMEM((PACK * TILE, R + TILE), F32)] * 4,
            *[pltpu.VMEM((PACK * TILE, R + TILE), BF16)] * 2,
            *[pltpu.VMEM((2 * KVH + 1, PACK * TILE, R + TILE), BF16)] * 2,
            pltpu.VMEM((2, DH, PACK * TILE), BF16),
            pltpu.VMEM((2, DH, PACK * TILE), BF16),
            pltpu.VMEM((2, DH, R), F32),
            pltpu.VMEM((2, DH, TILE), F32),
            pltpu.VMEM((3, PACK * TILE, DH), F32),
            pltpu.VMEM((KVH, NY, 2, NX, NZ // 2, 16, DH), BF16),
            pltpu.VMEM(half, BF16),
            pltpu.VMEM(half, BF16),
            pltpu.VMEM((KVH, NX * NY - 1, NZ // 2, 16, DH), BF16),
            pltpu.VMEM((KVH, NZ // 2, 16, DH), BF16),
            pltpu.VMEM((KVH, NZ - 1, 16, DH), BF16),
            pltpu.VMEM((KVH, 16, DH), F32),
            pltpu.VMEM((KVH, NX, 16, DH), F32),
            dma((5,)),
            dma,
            dma((CHUNKS,)),
            dma,
            dma((CHUNKS,)),
            dma,
            dma((CHUNKS,)),
            dma,
            dma((KVH,)),
            dma,
            dma((KVH,)),
            dma,
            dma((KVH,)),
            dma,
            dma((KVH,)),
        ],
        compiler_params=pltpu.CompilerParams(
            collective_id=0, has_side_effects=True, vmem_limit_bytes=48 << 20
        ),
    )(lengths, segments, query, grad_out, branch_kv, root_kv)


def solution(mesh):
    placed = (
        P(("grp", "dev"), None, None),
        P(("grp", "dev"), None, None),
        P(("grp", "dev"), None, None),
        P("dev", None),
        P(("grp", "dev")),
        P(("grp", "dev")),
    )
    return jax.shard_map(
        local,
        mesh=mesh,
        in_specs=placed,
        out_specs=(P(("grp", "dev"), None, None), P(("grp", "dev"), None, None), P("dev", None)),
        check_vma=False,
    )
```

```python
import functools
import math

import jax
import jax.numpy as jnp
from jax import lax
from jax.experimental import pallas as pl
from jax.experimental.pallas import tpu as pltpu
from jax.sharding import PartitionSpec as P

KVH = 4
GROUP = 8
DH = 128
TILE = 128
R = 1024
SEGS = 4
NX, NY, NZ = 4, 4, 8
CHUNKS = 2 * KVH
WIDTH = KVH * DH
SCALE = DH**-0.5
SCALE_LOG2 = SCALE * math.log2(math.e)
PACK = 4
ROWS = 16
AHEAD = 3

F32 = jnp.float32
BF16 = jnp.bfloat16
MESH = pl.DeviceIdType.MESH
NT = (((1,), (1,)), ((), ()))
NN = (((1,), (0,)), ((), ()))


def dot(a, b, dims):
    return lax.dot_general(a, b, dims, preferred_element_type=F32)


TILES = R // DH + 1
OF_PART = R // SEGS // DH


def tile_of(ref, first, b):
    return ref[pl.ds(first, ROWS), b * DH : (b + 1) * DH]


def across(x, reduce):
    return jnp.broadcast_to(reduce(x, axis=1, keepdims=True), (ROWS, DH))


def peaks(first, segment, s_ref, stats):
    row_pos = first % TILE + lax.broadcasted_iota(jnp.int32, (ROWS, DH), 0)
    col_pos = lax.broadcasted_iota(jnp.int32, (ROWS, DH), 1)
    branch = jnp.where(col_pos <= row_pos, tile_of(s_ref, first, TILES - 1), F32(-1e30))
    peak = branch
    for part in range(SEGS):
        top = tile_of(s_ref, first, part * OF_PART)
        for b in range(part * OF_PART + 1, (part + 1) * OF_PART):
            top = jnp.maximum(top, tile_of(s_ref, first, b))
        seen = top if part == 0 else jnp.where(part <= segment, top, F32(-1e30))
        peak = jnp.maximum(peak, seen)
    stats[0, pl.ds(first, ROWS)] = across(peak, jnp.max) * SCALE_LOG2


def exponentials(first, segment, s_ref, d_ref, stats):
    rows = pl.ds(first, ROWS)
    row_pos = first % TILE + lax.broadcasted_iota(jnp.int32, (ROWS, DH), 0)
    col_pos = lax.broadcasted_iota(jnp.int32, (ROWS, DH), 1)
    shift = stats[0, rows]
    total = delta = None
    for b in range(TILES):
        score = tile_of(s_ref, first, b)
        own_shift = shift
        if b == TILES - 1:
            own_shift = jnp.where(col_pos <= row_pos, shift, F32(1e30))
        elif b >= OF_PART:
            own_shift = jnp.where(b // OF_PART <= segment, shift, F32(1e30))
        e = jnp.exp2(score * SCALE_LOG2 - own_shift)
        s_ref[rows, b * DH : (b + 1) * DH] = e
        term = e * tile_of(d_ref, first, b)
        total = e if total is None else total + e
        delta = term if delta is None else delta + term
    inverse = 1.0 / across(total, jnp.sum)
    stats[1, rows] = inverse
    stats[2, rows] = across(delta, jnp.sum) * inverse


def weigh(first, s_ref, d_ref, p_ref, ds_ref, stats):
    rows = pl.ds(first, ROWS)
    inverse, delta = stats[1, rows], stats[2, rows]
    for b in range(TILES):
        cols = slice(b * DH, (b + 1) * DH)
        w = tile_of(s_ref, first, b) * inverse
        p_ref[rows, cols] = w.astype(BF16)
        ds_ref[rows, cols] = (w * (tile_of(d_ref, first, b) - delta)).astype(BF16)


def interleaved(many, few):
    done = 0
    for i, piece in enumerate(many):
        piece()
        while done < len(few) and (done + 1) * len(many) <= (i + 1) * len(few):
            few[done]()
            done += 1
    assert done == len(few)


def kernel(
    lengths_hbm,
    segments_hbm,
    q_hbm,
    g_hbm,
    branch_hbm,
    root_hbm,
    dq_ref,
    db_ref,
    out_ref,
    lengths,
    segments,
    q_s,
    g_s,
    branch_s,
    root_ref,
    kv,
    sa,
    sb,
    da,
    db,
    pa,
    pb,
    ds_a,
    ds_b,
    q_t,
    g_t,
    acc,
    branch_acc,
    stats,
    dpart,
    r0,
    s1,
    r1,
    s2,
    r2,
    s3,
    r3,
    in_sem,
    z_send,
    z_recv,
    y_send,
    y_recv,
    c_send,
    c_recv,
    s0_send,
    s0_recv,
    s1_send,
    s1_recv,
    s2_send,
    s2_recv,
    s3_send,
    s3_recv,
):
    grp = lax.axis_index("grp")
    dev = lax.axis_index("dev")
    x, z_lo = grp // 2, grp % 2
    y, z_hi, c = dev // 8, (dev // 2) % 4, dev % 2
    z = 2 * z_hi + z_lo

    def at(px, py, pz, pc):
        return (px * 2 + pz % 2, py * 8 + (pz // 2) * 2 + pc)

    def ring_z(offset):
        return (z + offset + NZ) % NZ

    away = 2 * z_lo - 1
    z_dests = [at(x, y, ring_z(away * k), c) for k in (1, 2, 3)]
    y_dests = [at(x, (y + k) % NY, z, c) for k in (1, 3)]
    y_from = [(y + k) % NY for k in (3, 1)]
    other_core = at(x, y, z, 1 - c)
    plane = [((x + k // NY) % NX, (y + k % NY) % NY) for k in range(1, NX * NY)]
    column = [(z + k) % NZ for k in range(1, NZ)]
    x_dests = [at((x + k) % NX, y, z, c) for k in (1, 2, 3)]

    q_copies = [pltpu.make_async_copy(q_hbm.at[t], q_s.at[t], in_sem.at[t]) for t in range(2)]
    g_copies = [pltpu.make_async_copy(g_hbm.at[t], g_s.at[t], in_sem.at[2 + t]) for t in range(2)]
    b_copy = pltpu.make_async_copy(branch_hbm, branch_s, in_sem.at[4])
    small = (
        pltpu.make_async_copy(lengths_hbm, lengths, in_sem.at[5]),
        pltpu.make_async_copy(segments_hbm, segments, in_sem.at[6]),
        pltpu.make_async_copy(root_hbm, root_ref, in_sem.at[7]),
    )
    for copy in (*small[::-1], b_copy, q_copies[0], g_copies[0], q_copies[1], g_copies[1]):
        copy.start()

    barrier = pltpu.get_barrier_semaphore()

    def greet(device):
        pl.semaphore_signal(barrier, inc=1, device_id=device, device_id_type=MESH)

    greet(other_core)
    for px, py in plane:
        greet(at(px, py, z, c))
    for pz in column:
        greet(at(x, y, pz, c))
    pl.semaphore_wait(barrier, 1 + len(plane) + len(column))

    def remote(src, dst, send_sem, recv_sem, device):
        return pltpu.make_async_remote_copy(
            src_ref=src,
            dst_ref=dst,
            send_sem=send_sem,
            recv_sem=recv_sem,
            device_id=device,
            device_id_type=MESH,
        )

    def arrived(ref, sem):
        pltpu.make_async_copy(ref, ref, sem).wait()

    def gather_z(chunk):
        start = (chunk % 2) * WIDTH + (chunk // 2) * DH
        src = root_ref.at[:, start : start + DH]
        dst = kv.at[chunk, y, c, z_hi]
        pltpu.make_async_copy(src, dst, z_recv.at[chunk]).start()
        for device in z_dests:
            remote(src, dst, z_send, z_recv.at[chunk], device).start()

    def to_core(chunk, py):
        block = kv.at[chunk, py, c]
        remote(block, block, c_send, c_recv.at[chunk], other_core).start()

    def gather_y(chunk):
        block = kv.at[chunk, y, c]
        arrived(block, z_recv.at[chunk])
        for side in range(2):
            remote(block, block, y_send, y_recv.at[chunk, side], y_dests[side]).start()
        to_core(chunk, y)

    def relay_y(chunk):
        for side in range(2):
            py = y_from[side]
            arrived(kv.at[chunk, py, c], y_recv.at[chunk, side])
            block = kv.at[chunk, py, c, pl.ds(2 * side, 2)]
            remote(block, block, y_send, y_recv.at[chunk, 2], y_dests[side]).start()
        for side in range(2):
            to_core(chunk, y_from[side])

    def gather_core(chunk):
        far = (y + 2) % NY
        arrived(kv.at[chunk, far, c], y_recv.at[chunk, 2])
        to_core(chunk, far)

    def gathered(chunk):
        arrived(kv.at[chunk, :, 1 - c], c_recv.at[chunk])

    def reduce_core(head, kind):
        both = pl.ds(2 * kind, 2)
        src, dst = dpart.at[head, :, 1 - c, both], r0.at[head, :, both]
        remote(src, dst, s0_send, s0_recv.at[head], other_core).start()

    def reduce_plane(head):
        arrived(r0.at[head], s0_recv.at[head])
        s1[head] = (dpart[head, :, c].astype(F32) + r0[head].astype(F32)).astype(BF16)
        for k, (px, py) in enumerate(plane):
            remote(
                s1.at[head, py, px], r1.at[head, k], s1_send, s1_recv.at[head], at(px, py, z, c)
            ).start()

    def reduce_column(head):
        arrived(r1.at[head], s1_recv.at[head])
        s2[head] = (s1[head, y, x].astype(F32) + jnp.sum(r1[head].astype(F32), axis=0)).astype(BF16)
        for k, pz in enumerate(column):
            remote(
                s2.at[head, pz // 2], r2.at[head, k], s2_send, s2_recv.at[head], at(x, y, pz, c)
            ).start()

    def share_sum(head):
        arrived(r2.at[head], s2_recv.at[head])
        summed = s2[head, z_hi].astype(F32) + jnp.sum(r2[head].astype(F32), axis=0)
        s3[head] = summed
        r3[head, x] = summed
        for device in x_dests:
            remote(s3.at[head], r3.at[head, x], s3_send, s3_recv.at[head], device).start()

    def reduce_done(head):
        arrived(r3.at[head, pl.ds(0, 3)], s3_recv.at[head])
        for part in range(NX):
            cols = pl.ds(pl.multiple_of((part // 2) * WIDTH + head * DH, DH), DH)
            out_ref[(part % 2) * 16 : (part % 2 + 1) * 16, cols] = r3[head, part]

    ds_s = (ds_a, ds_b)

    def columns(first, count=1):
        return pl.ds(pl.multiple_of(first * DH, DH), count * DH)

    def scores_of(index, pack, s_ref, d_ref):
        head, t = index // 2, index % 2
        live = lax.broadcasted_iota(jnp.int32, (TILE, DH), 0) < lengths[t]
        first = head * GROUP + pack * PACK
        qs = [q_s[t, :, columns(first + j)] for j in range(PACK)]
        gs = [
            jnp.where(live, g_s[t, :, columns(first + j)], jnp.zeros((), BF16)) for j in range(PACK)
        ]
        q, g = jnp.concatenate(qs, axis=0), jnp.concatenate(gs, axis=0)

        def turn():
            for j in range(PACK):
                q_t[pack, :, j * TILE : (j + 1) * TILE] = qs[j].T
                g_t[pack, :, j * TILE : (j + 1) * TILE] = gs[j].T

        def root(of, ref, chunk, b):
            part = kv[chunk, b].reshape(R // SEGS, DH)
            ref[:, b * R // SEGS : (b + 1) * R // SEGS] = dot(of, part, NT)

        def branch(of, ref, start):
            ref[:, R:] = dot(of, branch_s[t, :, columns(start + head)], NT)

        pieces = []
        for of, ref, kind in ((q, s_ref, 0), (g, d_ref, 1)):
            pieces += [functools.partial(root, of, ref, 2 * head + kind, b) for b in range(SEGS)]
            pieces.append(functools.partial(branch, of, ref, kind * KVH))
        return pieces + [turn]

    def key_grads(index, pack, p_ref, is_first):
        part = R // SEGS

        def root(kind, ref, rows_t, b):
            cols = slice(b * part, (b + 1) * part)
            acc[kind, :, cols] = acc[kind, :, cols] + dot(rows_t[pack], ref[:, cols], NN)

        def branch(kind, ref, rows_t):
            term = dot(rows_t[pack], ref[:, R:], NN)
            branch_acc[kind] = term if is_first else branch_acc[kind] + term

        pieces = []
        for kind, ref, rows_t in ((1, p_ref, g_t), (0, ds_s[pack].at[index], q_t)):
            pieces += [functools.partial(root, kind, ref, rows_t, b) for b in range(SEGS)]
            pieces.append(functools.partial(branch, kind, ref, rows_t))
        return pieces

    def softmax_of(index, pack, s_ref, d_ref, p_ref):
        segment = segments[index % 2]
        ds_ref = ds_s[pack].at[index]
        count = PACK * TILE // ROWS

        def piece(i):
            if i + 2 * AHEAD < count:
                peaks((i + 2 * AHEAD) * ROWS, segment, s_ref, stats)
            if 0 <= i + AHEAD < count:
                exponentials((i + AHEAD) * ROWS, segment, s_ref, d_ref, stats)
            if i >= 0:
                weigh(i * ROWS, s_ref, d_ref, p_ref, ds_ref, stats)

        return [functools.partial(piece, i) for i in range(-2 * AHEAD, count)]

    def put_branch(index):
        head, t = index // 2, index % 2
        db_ref[t, :, columns(head)] = (branch_acc[0].T * SCALE).astype(BF16)
        db_ref[t, :, columns(KVH + head)] = branch_acc[1].T.astype(BF16)

    def put_root(head):
        shape = (NY, 2, NZ // 2, 2, 16, DH)
        for kind in (1, 0):
            rows = acc[kind].T
            rows = (rows * SCALE if kind == 0 else rows).astype(BF16).reshape(shape)
            for half in range(2):
                dpart[head, :, :, 2 * kind + half] = rows[:, :, :, half]
            reduce_core(head, kind)
        acc[...] = jnp.zeros_like(acc)

    for copy in small:
        copy.wait()
    for chunk in range(CHUNKS):
        gather_z(chunk)
    for chunk in range(2):
        gather_y(chunk)
    acc[...] = jnp.zeros_like(acc)
    branch_acc[...] = jnp.zeros_like(branch_acc)
    q_t[1] = jnp.zeros_like(q_t[1])
    g_t[1] = jnp.zeros_like(g_t[1])
    pb[...] = jnp.zeros_like(pb)
    ds_b[2 * KVH] = jnp.zeros_like(pb)
    for chunk in range(2):
        relay_y(chunk)
    for chunk in range(2, CHUNKS):
        gather_y(chunk)
    for chunk in range(2):
        gather_core(chunk)
    b_copy.wait()
    q_copies[0].wait()
    g_copies[0].wait()
    gathered(0)
    gathered(1)
    for piece in scores_of(0, 0, sa, da):
        piece()

    def step(index, carry, final=False):
        head, t = index // 2, index % 2
        before = jnp.where(index == 0, 2 * KVH, index - 1)
        after = index + 1

        @pl.when(index == 0)
        def _():
            q_copies[1].wait()
            g_copies[1].wait()

        @pl.when(jnp.logical_and(t == 0, head < KVH - 1))
        def _():
            relay_y(2 * head + 2)
            relay_y(2 * head + 3)

        interleaved(
            softmax_of(index, 0, sa, da, pa),
            key_grads(before, 1, pb, False) + scores_of(index, 1, sb, db),
        )

        @pl.when(index > 0)
        def _():
            put_branch(before)

        @pl.when(jnp.logical_and(t == 0, head >= 1))
        def _():
            put_root(head - 1)

        @pl.when(jnp.logical_and(t == 0, head < KVH - 1))
        def _():
            gather_core(2 * head + 2)
            gather_core(2 * head + 3)

        @pl.when(jnp.logical_and(t == 1, head < KVH - 1))
        def _():
            gathered(2 * head + 2)
            gathered(2 * head + 3)

        @pl.when(jnp.logical_and(t == 1, head >= 1))
        def _():
            reduce_plane(head - 1)

        @pl.when(jnp.logical_and(t == 1, head >= 2))
        def _():
            reduce_column(head - 2)

        interleaved(
            softmax_of(index, 1, sb, db, pb),
            key_grads(index, 0, pa, True) + ([] if final else scores_of(after, 0, sa, da)),
        )

        @pl.when(jnp.logical_and(t == 0, head == KVH - 1))
        def _():
            share_sum(head - 3)

        return carry

    def query_grads(index, carry):
        head, t = index // 2, index % 2
        k_cols = pl.ds(pl.multiple_of(head * DH, DH), DH)
        for pack in range(2):
            rows = ds_s[pack].at[index]
            dq = dot(rows[:, :R], kv[2 * head].reshape(R, DH), NN)
            dq = dq + dot(rows[:, R:], branch_s[t, :, k_cols], NN)
            dq = (dq * SCALE).astype(BF16)
            for j in range(PACK):
                cols = columns(head * GROUP + pack * PACK + j)
                dq_ref[t, :, cols] = dq[j * TILE : (j + 1) * TILE]
        return carry

    last = KVH - 1
    lax.fori_loop(0, 2 * KVH - 1, step, 0)
    step(jnp.int32(2 * KVH - 1), 0, final=True)
    for piece in key_grads(2 * KVH - 1, 1, pb, False):
        piece()
    put_root(last)
    put_branch(2 * KVH - 1)
    reduce_column(last - 1)
    lax.fori_loop(0, 1, query_grads, 0)
    reduce_plane(last)
    share_sum(last - 2)
    reduce_done(last - 3)
    lax.fori_loop(1, 5, query_grads, 0)
    share_sum(last - 1)
    reduce_column(last)
    reduce_done(last - 2)
    lax.fori_loop(5, 8, query_grads, 0)
    reduce_done(last - 1)
    share_sum(last)
    reduce_done(last)

    for _ in range(3):
        arrived(kv.at[:, 0, 0, 0], z_send)
        arrived(kv.at[:, 0, 0], y_send)
    arrived(kv.at[:, :, 0], c_send)
    arrived(r0, s0_send)
    arrived(r1, s1_send)
    arrived(r2, s2_send)
    arrived(r3.at[:, pl.ds(0, 3)], s3_send)


def local(query, grad_out, branch_kv, root_kv, lengths, segments):
    rows = R // 32
    hbm = pl.BlockSpec(memory_space=pltpu.HBM)
    vmem = pl.BlockSpec(memory_space=pltpu.VMEM)
    dma = pltpu.SemaphoreType.DMA
    blocks = (CHUNKS, NY, 2, NZ // 2, rows, DH)
    half = (KVH, NY, NX, NZ // 2, 16, DH)
    return pl.pallas_call(
        kernel,
        out_shape=(
            jax.ShapeDtypeStruct(query.shape, BF16),
            jax.ShapeDtypeStruct(branch_kv.shape, BF16),
            jax.ShapeDtypeStruct(root_kv.shape, F32),
        ),
        in_specs=[hbm] * 6,
        out_specs=(vmem, vmem, vmem),
        scratch_shapes=[
            pltpu.SMEM(lengths.shape, jnp.int32),
            pltpu.SMEM(segments.shape, jnp.int32),
            pltpu.VMEM(query.shape, BF16),
            pltpu.VMEM(query.shape, BF16),
            pltpu.VMEM(branch_kv.shape, BF16),
            pltpu.VMEM(root_kv.shape, BF16),
            pltpu.VMEM(blocks, BF16),
            *[pltpu.VMEM((PACK * TILE, R + TILE), F32)] * 4,
            *[pltpu.VMEM((PACK * TILE, R + TILE), BF16)] * 2,
            *[pltpu.VMEM((2 * KVH + 1, PACK * TILE, R + TILE), BF16)] * 2,
            pltpu.VMEM((2, DH, PACK * TILE), BF16),
            pltpu.VMEM((2, DH, PACK * TILE), BF16),
            pltpu.VMEM((2, DH, R), F32),
            pltpu.VMEM((2, DH, TILE), F32),
            pltpu.VMEM((3, PACK * TILE, DH), F32),
            pltpu.VMEM((KVH, NY, 2, NX, NZ // 2, 16, DH), BF16),
            pltpu.VMEM(half, BF16),
            pltpu.VMEM(half, BF16),
            pltpu.VMEM((KVH, NX * NY - 1, NZ // 2, 16, DH), BF16),
            pltpu.VMEM((KVH, NZ // 2, 16, DH), BF16),
            pltpu.VMEM((KVH, NZ - 1, 16, DH), BF16),
            pltpu.VMEM((KVH, 16, DH), F32),
            pltpu.VMEM((KVH, NX, 16, DH), F32),
            dma((8,)),
            dma,
            dma((CHUNKS,)),
            dma,
            dma((CHUNKS, 3)),
            dma,
            dma((CHUNKS,)),
            dma,
            dma((KVH,)),
            dma,
            dma((KVH,)),
            dma,
            dma((KVH,)),
            dma,
            dma((KVH,)),
        ],
        compiler_params=pltpu.CompilerParams(
            collective_id=0, has_side_effects=True, vmem_limit_bytes=49 << 20
        ),
    )(*[pltpu.with_memory_space_constraint(a, pltpu.HBM) for a in (lengths, segments, query, grad_out, branch_kv, root_kv)])


def solution(mesh):
    placed = (
        P(("grp", "dev"), None, None),
        P(("grp", "dev"), None, None),
        P(("grp", "dev"), None, None),
        P("dev", None),
        P(("grp", "dev")),
        P(("grp", "dev")),
    )
    return jax.shard_map(
        local,
        mesh=mesh,
        in_specs=placed,
        out_specs=(P(("grp", "dev"), None, None), P(("grp", "dev"), None, None), P("dev", None)),
        check_vma=False,
    )
```

```python
import functools
import math

import jax
import jax.numpy as jnp
from jax import lax
from jax.experimental import pallas as pl
from jax.experimental.pallas import tpu as pltpu
from jax.sharding import PartitionSpec as P

KVH = 4
GROUP = 8
DH = 128
TILE = 128
R = 1024
SEGS = 4
NX, NY, NZ = 4, 4, 8
CHUNKS = 2 * KVH
WIDTH = KVH * DH
SCALE = DH**-0.5
SCALE_LOG2 = SCALE * math.log2(math.e)
PACK = 4
ROWS = 16
AHEAD = 3

F32 = jnp.float32
BF16 = jnp.bfloat16
MESH = pl.DeviceIdType.MESH
NT = (((1,), (1,)), ((), ()))
NN = (((1,), (0,)), ((), ()))


def dot(a, b, dims):
    return lax.dot_general(a, b, dims, preferred_element_type=F32)


TILES = R // DH + 1
OF_PART = R // SEGS // DH


def tile_of(ref, first, b):
    return ref[pl.ds(first, ROWS), b * DH : (b + 1) * DH]


def across(x, reduce):
    return jnp.broadcast_to(reduce(x, axis=1, keepdims=True), (ROWS, DH))


def peaks(first, segment, s_ref, stats):
    row_pos = first % TILE + lax.broadcasted_iota(jnp.int32, (ROWS, DH), 0)
    col_pos = lax.broadcasted_iota(jnp.int32, (ROWS, DH), 1)
    branch = jnp.where(col_pos <= row_pos, tile_of(s_ref, first, TILES - 1), F32(-1e30))
    peak = branch
    for part in range(SEGS):
        top = tile_of(s_ref, first, part * OF_PART)
        for b in range(part * OF_PART + 1, (part + 1) * OF_PART):
            top = jnp.maximum(top, tile_of(s_ref, first, b))
        seen = top if part == 0 else jnp.where(part <= segment, top, F32(-1e30))
        peak = jnp.maximum(peak, seen)
    stats[0, pl.ds(first, ROWS)] = across(peak, jnp.max) * SCALE_LOG2


def exponentials(first, segment, s_ref, d_ref, stats):
    rows = pl.ds(first, ROWS)
    row_pos = first % TILE + lax.broadcasted_iota(jnp.int32, (ROWS, DH), 0)
    col_pos = lax.broadcasted_iota(jnp.int32, (ROWS, DH), 1)
    shift = stats[0, rows]
    total = delta = None
    for b in range(TILES):
        score = tile_of(s_ref, first, b)
        own_shift = shift
        if b == TILES - 1:
            own_shift = jnp.where(col_pos <= row_pos, shift, F32(1e30))
        elif b >= OF_PART:
            own_shift = jnp.where(b // OF_PART <= segment, shift, F32(1e30))
        e = jnp.exp2(score * SCALE_LOG2 - own_shift)
        s_ref[rows, b * DH : (b + 1) * DH] = e
        term = e * tile_of(d_ref, first, b)
        total = e if total is None else total + e
        delta = term if delta is None else delta + term
    inverse = 1.0 / across(total, jnp.sum)
    stats[1, rows] = inverse
    stats[2, rows] = across(delta, jnp.sum) * inverse


def weigh(first, s_ref, d_ref, p_ref, ds_ref, stats):
    rows = pl.ds(first, ROWS)
    inverse, delta = stats[1, rows], stats[2, rows]
    for b in range(TILES):
        cols = slice(b * DH, (b + 1) * DH)
        w = tile_of(s_ref, first, b) * inverse
        p_ref[rows, cols] = w.astype(BF16)
        ds_ref[rows, cols] = (w * (tile_of(d_ref, first, b) - delta)).astype(BF16)


def interleaved(many, few):
    done = 0
    for i, piece in enumerate(many):
        piece()
        while done < len(few) and (done + 1) * len(many) <= (i + 1) * len(few):
            few[done]()
            done += 1
    assert done == len(few)


def kernel(
    lengths_hbm,
    segments_hbm,
    q_hbm,
    g_hbm,
    branch_hbm,
    root_hbm,
    dq_ref,
    db_ref,
    out_ref,
    lengths,
    segments,
    q_s,
    g_s,
    branch_s,
    root_ref,
    kv,
    sa,
    sb,
    da,
    db,
    pa,
    pb,
    ds_a,
    ds_b,
    q_t,
    g_t,
    acc,
    branch_acc,
    stats,
    dpart,
    r0,
    s1,
    r1,
    s2,
    r2,
    s3,
    r3,
    in_sem,
    z_send,
    z_recv,
    y_send,
    y_recv,
    c_send,
    c_recv,
    s0_send,
    s0_recv,
    s1_send,
    s1_recv,
    s2_send,
    s2_recv,
    s3_send,
    s3_recv,
):
    grp = lax.axis_index("grp")
    dev = lax.axis_index("dev")
    x, z_lo = grp // 2, grp % 2
    y, z_hi, c = dev // 8, (dev // 2) % 4, dev % 2
    z = 2 * z_hi + z_lo

    def at(px, py, pz, pc):
        return (px * 2 + pz % 2, py * 8 + (pz // 2) * 2 + pc)

    def ring_z(offset):
        return (z + offset + NZ) % NZ

    away = 2 * z_lo - 1
    z_dests = [at(x, y, ring_z(away * k), c) for k in (1, 2, 3)]
    y_dests = [at(x, (y + k) % NY, z, c) for k in (1, 2, 3)]
    other_core = at(x, y, z, 1 - c)
    plane = [((x + k // NY) % NX, (y + k % NY) % NY) for k in range(1, NX * NY)]
    column = [(z + k) % NZ for k in range(1, NZ)]
    x_dests = [at((x + k) % NX, y, z, c) for k in (1, 2, 3)]

    q_copies = [pltpu.make_async_copy(q_hbm.at[t], q_s.at[t], in_sem.at[t]) for t in range(2)]
    g_copies = [pltpu.make_async_copy(g_hbm.at[t], g_s.at[t], in_sem.at[2 + t]) for t in range(2)]
    b_copy = pltpu.make_async_copy(branch_hbm, branch_s, in_sem.at[4])
    small = (
        pltpu.make_async_copy(lengths_hbm, lengths, in_sem.at[5]),
        pltpu.make_async_copy(segments_hbm, segments, in_sem.at[6]),
        pltpu.make_async_copy(root_hbm, root_ref, in_sem.at[7]),
    )
    for copy in (*small[::-1], b_copy, q_copies[0], g_copies[0], q_copies[1], g_copies[1]):
        copy.start()

    barrier = pltpu.get_barrier_semaphore()

    def greet(device):
        pl.semaphore_signal(barrier, inc=1, device_id=device, device_id_type=MESH)

    greet(other_core)
    for px, py in plane:
        greet(at(px, py, z, c))
    for pz in column:
        greet(at(x, y, pz, c))
    pl.semaphore_wait(barrier, 1 + len(plane) + len(column))

    def remote(src, dst, send_sem, recv_sem, device):
        return pltpu.make_async_remote_copy(
            src_ref=src,
            dst_ref=dst,
            send_sem=send_sem,
            recv_sem=recv_sem,
            device_id=device,
            device_id_type=MESH,
        )

    def arrived(ref, sem):
        pltpu.make_async_copy(ref, ref, sem).wait()

    def gather_z(chunk):
        start = (chunk % 2) * WIDTH + (chunk // 2) * DH
        src = root_ref.at[:, start : start + DH]
        dst = kv.at[chunk, y, c, z_hi]
        pltpu.make_async_copy(src, dst, z_recv.at[chunk]).start()
        for device in z_dests:
            remote(src, dst, z_send, z_recv.at[chunk], device).start()

    def gather_y(chunk):
        block = kv.at[chunk, y, c]
        arrived(block, z_recv.at[chunk])
        for device in y_dests:
            remote(block, block, y_send, y_recv.at[chunk], device).start()

    def gather_core(chunk):
        arrived(kv.at[chunk, pl.ds(0, 3), c], y_recv.at[chunk])
        block = kv.at[chunk, :, c]
        remote(block, block, c_send, c_recv.at[chunk], other_core).start()

    def gathered(chunk):
        arrived(kv.at[chunk, :, 1 - c], c_recv.at[chunk])

    def reduce_core(head, kind):
        both = pl.ds(2 * kind, 2)
        src, dst = dpart.at[head, :, 1 - c, both], r0.at[head, :, both]
        remote(src, dst, s0_send, s0_recv.at[head], other_core).start()

    def reduce_plane(head):
        arrived(r0.at[head], s0_recv.at[head])
        s1[head] = (dpart[head, :, c].astype(F32) + r0[head].astype(F32)).astype(BF16)
        for k, (px, py) in enumerate(plane):
            remote(
                s1.at[head, py, px], r1.at[head, k], s1_send, s1_recv.at[head], at(px, py, z, c)
            ).start()

    def reduce_column(head):
        arrived(r1.at[head], s1_recv.at[head])
        s2[head] = (s1[head, y, x].astype(F32) + jnp.sum(r1[head].astype(F32), axis=0)).astype(BF16)
        for k, pz in enumerate(column):
            remote(
                s2.at[head, pz // 2], r2.at[head, k], s2_send, s2_recv.at[head], at(x, y, pz, c)
            ).start()

    def share_sum(head):
        arrived(r2.at[head], s2_recv.at[head])
        summed = s2[head, z_hi].astype(F32) + jnp.sum(r2[head].astype(F32), axis=0)
        s3[head] = summed
        r3[head, x] = summed
        for device in x_dests:
            remote(s3.at[head], r3.at[head, x], s3_send, s3_recv.at[head], device).start()

    def reduce_done(head):
        arrived(r3.at[head, pl.ds(0, 3)], s3_recv.at[head])
        for part in range(NX):
            cols = pl.ds(pl.multiple_of((part // 2) * WIDTH + head * DH, DH), DH)
            out_ref[(part % 2) * 16 : (part % 2 + 1) * 16, cols] = r3[head, part]

    ds_s = (ds_a, ds_b)

    def columns(first, count=1):
        return pl.ds(pl.multiple_of(first * DH, DH), count * DH)

    def scores_of(index, pack, s_ref, d_ref):
        head, t = index // 2, index % 2
        live = lax.broadcasted_iota(jnp.int32, (TILE, DH), 0) < lengths[t]
        first = head * GROUP + pack * PACK
        qs = [q_s[t, :, columns(first + j)] for j in range(PACK)]
        gs = [
            jnp.where(live, g_s[t, :, columns(first + j)], jnp.zeros((), BF16)) for j in range(PACK)
        ]
        q, g = jnp.concatenate(qs, axis=0), jnp.concatenate(gs, axis=0)

        def turn():
            for j in range(PACK):
                q_t[pack, :, j * TILE : (j + 1) * TILE] = qs[j].T
                g_t[pack, :, j * TILE : (j + 1) * TILE] = gs[j].T

        def root(of, ref, chunk, b):
            part = kv[chunk, b].reshape(R // SEGS, DH)
            ref[:, b * R // SEGS : (b + 1) * R // SEGS] = dot(of, part, NT)

        def branch(of, ref, start):
            ref[:, R:] = dot(of, branch_s[t, :, columns(start + head)], NT)

        pieces = []
        for of, ref, kind in ((q, s_ref, 0), (g, d_ref, 1)):
            pieces += [functools.partial(root, of, ref, 2 * head + kind, b) for b in range(SEGS)]
            pieces.append(functools.partial(branch, of, ref, kind * KVH))
        return pieces + [turn]

    def key_grads(index, pack, p_ref, is_first):
        part = R // SEGS

        def root(kind, ref, rows_t, b):
            cols = slice(b * part, (b + 1) * part)
            acc[kind, :, cols] = acc[kind, :, cols] + dot(rows_t[pack], ref[:, cols], NN)

        def branch(kind, ref, rows_t):
            term = dot(rows_t[pack], ref[:, R:], NN)
            branch_acc[kind] = term if is_first else branch_acc[kind] + term

        pieces = []
        for kind, ref, rows_t in ((1, p_ref, g_t), (0, ds_s[pack].at[index], q_t)):
            pieces += [functools.partial(root, kind, ref, rows_t, b) for b in range(SEGS)]
            pieces.append(functools.partial(branch, kind, ref, rows_t))
        return pieces

    def softmax_of(index, pack, s_ref, d_ref, p_ref):
        segment = segments[index % 2]
        ds_ref = ds_s[pack].at[index]
        count = PACK * TILE // ROWS

        def piece(i):
            if i + 2 * AHEAD < count:
                peaks((i + 2 * AHEAD) * ROWS, segment, s_ref, stats)
            if 0 <= i + AHEAD < count:
                exponentials((i + AHEAD) * ROWS, segment, s_ref, d_ref, stats)
            if i >= 0:
                weigh(i * ROWS, s_ref, d_ref, p_ref, ds_ref, stats)

        return [functools.partial(piece, i) for i in range(-2 * AHEAD, count)]

    def put_branch(index):
        head, t = index // 2, index % 2
        db_ref[t, :, columns(head)] = (branch_acc[0].T * SCALE).astype(BF16)
        db_ref[t, :, columns(KVH + head)] = branch_acc[1].T.astype(BF16)

    def put_root(head):
        shape = (NY, 2, NZ // 2, 2, 16, DH)
        for kind in (1, 0):
            rows = acc[kind].T
            rows = (rows * SCALE if kind == 0 else rows).astype(BF16).reshape(shape)
            for half in range(2):
                dpart[head, :, :, 2 * kind + half] = rows[:, :, :, half]
            reduce_core(head, kind)
        acc[...] = jnp.zeros_like(acc)

    for copy in small:
        copy.wait()
    for chunk in range(CHUNKS):
        gather_z(chunk)
    for chunk in range(2):
        gather_y(chunk)
    acc[...] = jnp.zeros_like(acc)
    branch_acc[...] = jnp.zeros_like(branch_acc)
    q_t[1] = jnp.zeros_like(q_t[1])
    g_t[1] = jnp.zeros_like(g_t[1])
    pb[...] = jnp.zeros_like(pb)
    ds_b[2 * KVH] = jnp.zeros_like(pb)
    for chunk in range(2):
        gather_core(chunk)
    for chunk in range(2, 4):
        gather_y(chunk)
    b_copy.wait()
    q_copies[0].wait()
    g_copies[0].wait()
    gathered(0)
    gathered(1)
    for piece in scores_of(0, 0, sa, da):
        piece()

    def step(index, carry, final=False):
        head, t = index // 2, index % 2
        before = jnp.where(index == 0, 2 * KVH, index - 1)
        after = index + 1

        @pl.when(index == 0)
        def _():
            q_copies[1].wait()
            g_copies[1].wait()
            for chunk in range(4, CHUNKS):
                gather_y(chunk)

        interleaved(
            softmax_of(index, 0, sa, da, pa),
            key_grads(before, 1, pb, False) + scores_of(index, 1, sb, db),
        )

        @pl.when(index > 0)
        def _():
            put_branch(before)

        @pl.when(jnp.logical_and(t == 0, head >= 1))
        def _():
            put_root(head - 1)

        @pl.when(jnp.logical_and(t == 0, head < KVH - 1))
        def _():
            gather_core(2 * head + 2)
            gather_core(2 * head + 3)

        @pl.when(jnp.logical_and(t == 1, head < KVH - 1))
        def _():
            gathered(2 * head + 2)
            gathered(2 * head + 3)

        @pl.when(jnp.logical_and(t == 1, head >= 1))
        def _():
            reduce_plane(head - 1)

        @pl.when(jnp.logical_and(t == 1, head >= 2))
        def _():
            reduce_column(head - 2)

        interleaved(
            softmax_of(index, 1, sb, db, pb),
            key_grads(index, 0, pa, True) + ([] if final else scores_of(after, 0, sa, da)),
        )

        @pl.when(jnp.logical_and(t == 0, head == KVH - 1))
        def _():
            share_sum(head - 3)

        return carry

    def query_grads(index, carry):
        head, t = index // 2, index % 2
        k_cols = pl.ds(pl.multiple_of(head * DH, DH), DH)
        for pack in range(2):
            rows = ds_s[pack].at[index]
            dq = dot(rows[:, :R], kv[2 * head].reshape(R, DH), NN)
            dq = dq + dot(rows[:, R:], branch_s[t, :, k_cols], NN)
            dq = (dq * SCALE).astype(BF16)
            for j in range(PACK):
                cols = columns(head * GROUP + pack * PACK + j)
                dq_ref[t, :, cols] = dq[j * TILE : (j + 1) * TILE]
        return carry

    last = KVH - 1
    lax.fori_loop(0, 2 * KVH - 1, step, 0)
    step(jnp.int32(2 * KVH - 1), 0, final=True)
    for piece in key_grads(2 * KVH - 1, 1, pb, False):
        piece()
    put_root(last)
    put_branch(2 * KVH - 1)
    reduce_column(last - 1)
    lax.fori_loop(0, 1, query_grads, 0)
    reduce_plane(last)
    share_sum(last - 2)
    reduce_done(last - 3)
    lax.fori_loop(1, 5, query_grads, 0)
    share_sum(last - 1)
    reduce_column(last)
    reduce_done(last - 2)
    lax.fori_loop(5, 8, query_grads, 0)
    reduce_done(last - 1)
    share_sum(last)
    reduce_done(last)

    for _ in range(3):
        arrived(kv.at[:, 0, 0, 0], z_send)
        arrived(kv.at[:, 0, 0], y_send)
    arrived(kv.at[:, :, 0], c_send)
    arrived(r0, s0_send)
    arrived(r1, s1_send)
    arrived(r2, s2_send)
    arrived(r3.at[:, pl.ds(0, 3)], s3_send)


def local(query, grad_out, branch_kv, root_kv, lengths, segments):
    rows = R // 32
    hbm = pl.BlockSpec(memory_space=pltpu.HBM)
    vmem = pl.BlockSpec(memory_space=pltpu.VMEM)
    dma = pltpu.SemaphoreType.DMA
    blocks = (CHUNKS, NY, 2, NZ // 2, rows, DH)
    half = (KVH, NY, NX, NZ // 2, 16, DH)
    return pl.pallas_call(
        kernel,
        out_shape=(
            jax.ShapeDtypeStruct(query.shape, BF16),
            jax.ShapeDtypeStruct(branch_kv.shape, BF16),
            jax.ShapeDtypeStruct(root_kv.shape, F32),
        ),
        in_specs=[hbm] * 6,
        out_specs=(vmem, vmem, vmem),
        scratch_shapes=[
            pltpu.SMEM(lengths.shape, jnp.int32),
            pltpu.SMEM(segments.shape, jnp.int32),
            pltpu.VMEM(query.shape, BF16),
            pltpu.VMEM(query.shape, BF16),
            pltpu.VMEM(branch_kv.shape, BF16),
            pltpu.VMEM(root_kv.shape, BF16),
            pltpu.VMEM(blocks, BF16),
            *[pltpu.VMEM((PACK * TILE, R + TILE), F32)] * 4,
            *[pltpu.VMEM((PACK * TILE, R + TILE), BF16)] * 2,
            *[pltpu.VMEM((2 * KVH + 1, PACK * TILE, R + TILE), BF16)] * 2,
            pltpu.VMEM((2, DH, PACK * TILE), BF16),
            pltpu.VMEM((2, DH, PACK * TILE), BF16),
            pltpu.VMEM((2, DH, R), F32),
            pltpu.VMEM((2, DH, TILE), F32),
            pltpu.VMEM((3, PACK * TILE, DH), F32),
            pltpu.VMEM((KVH, NY, 2, NX, NZ // 2, 16, DH), BF16),
            pltpu.VMEM(half, BF16),
            pltpu.VMEM(half, BF16),
            pltpu.VMEM((KVH, NX * NY - 1, NZ // 2, 16, DH), BF16),
            pltpu.VMEM((KVH, NZ // 2, 16, DH), BF16),
            pltpu.VMEM((KVH, NZ - 1, 16, DH), BF16),
            pltpu.VMEM((KVH, 16, DH), F32),
            pltpu.VMEM((KVH, NX, 16, DH), F32),
            dma((8,)),
            dma,
            dma((CHUNKS,)),
            dma,
            dma((CHUNKS,)),
            dma,
            dma((CHUNKS,)),
            dma,
            dma((KVH,)),
            dma,
            dma((KVH,)),
            dma,
            dma((KVH,)),
            dma,
            dma((KVH,)),
        ],
        compiler_params=pltpu.CompilerParams(
            collective_id=0, has_side_effects=True, vmem_limit_bytes=49 << 20
        ),
    )(*[pltpu.with_memory_space_constraint(a, pltpu.HBM) for a in (lengths, segments, query, grad_out, branch_kv, root_kv)])


def solution(mesh):
    placed = (
        P(("grp", "dev"), None, None),
        P(("grp", "dev"), None, None),
        P(("grp", "dev"), None, None),
        P("dev", None),
        P(("grp", "dev")),
        P(("grp", "dev")),
    )
    return jax.shard_map(
        local,
        mesh=mesh,
        in_specs=placed,
        out_specs=(P(("grp", "dev"), None, None), P(("grp", "dev"), None, None), P("dev", None)),
        check_vma=False,
    )
```

```python
import functools
import math

import jax
import jax.numpy as jnp
from jax import lax
from jax.experimental import pallas as pl
from jax.experimental.pallas import tpu as pltpu
from jax.sharding import PartitionSpec as P

KVH = 4
GROUP = 8
DH = 128
TILE = 128
R = 1024
SEGS = 4
NX, NY, NZ = 4, 4, 8
CHUNKS = 2 * KVH
WIDTH = KVH * DH
SCALE = DH**-0.5
SCALE_LOG2 = SCALE * math.log2(math.e)
PACK = 4
ROWS = 16
AHEAD = 3

F32 = jnp.float32
BF16 = jnp.bfloat16
MESH = pl.DeviceIdType.MESH
NT = (((1,), (1,)), ((), ()))
NN = (((1,), (0,)), ((), ()))


def dot(a, b, dims):
    return lax.dot_general(a, b, dims, preferred_element_type=F32)


TILES = R // DH + 1
OF_PART = R // SEGS // DH


def tile_of(ref, first, b):
    return ref[pl.ds(first, ROWS), b * DH : (b + 1) * DH]


def across(x, reduce):
    return jnp.broadcast_to(reduce(x, axis=1, keepdims=True), (ROWS, DH))


def peaks(first, segment, s_ref, stats):
    row_pos = first % TILE + lax.broadcasted_iota(jnp.int32, (ROWS, DH), 0)
    col_pos = lax.broadcasted_iota(jnp.int32, (ROWS, DH), 1)
    branch = jnp.where(col_pos <= row_pos, tile_of(s_ref, first, TILES - 1), F32(-1e30))
    peak = branch
    for part in range(SEGS):
        top = tile_of(s_ref, first, part * OF_PART)
        for b in range(part * OF_PART + 1, (part + 1) * OF_PART):
            top = jnp.maximum(top, tile_of(s_ref, first, b))
        seen = top if part == 0 else jnp.where(part <= segment, top, F32(-1e30))
        peak = jnp.maximum(peak, seen)
    stats[0, pl.ds(first, ROWS)] = across(peak, jnp.max) * SCALE_LOG2


def exponentials(first, segment, s_ref, d_ref, stats):
    rows = pl.ds(first, ROWS)
    row_pos = first % TILE + lax.broadcasted_iota(jnp.int32, (ROWS, DH), 0)
    col_pos = lax.broadcasted_iota(jnp.int32, (ROWS, DH), 1)
    shift = stats[0, rows]
    total = delta = None
    for b in range(TILES):
        score = tile_of(s_ref, first, b)
        own_shift = shift
        if b == TILES - 1:
            own_shift = jnp.where(col_pos <= row_pos, shift, F32(1e30))
        elif b >= OF_PART:
            own_shift = jnp.where(b // OF_PART <= segment, shift, F32(1e30))
        e = jnp.exp2(score * SCALE_LOG2 - own_shift)
        s_ref[rows, b * DH : (b + 1) * DH] = e
        term = e * tile_of(d_ref, first, b)
        total = e if total is None else total + e
        delta = term if delta is None else delta + term
    inverse = 1.0 / across(total, jnp.sum)
    stats[1, rows] = inverse
    stats[2, rows] = across(delta, jnp.sum) * inverse


def weigh(first, s_ref, d_ref, p_ref, ds_ref, stats):
    rows = pl.ds(first, ROWS)
    inverse, delta = stats[1, rows], stats[2, rows]
    for b in range(TILES):
        cols = slice(b * DH, (b + 1) * DH)
        w = tile_of(s_ref, first, b) * inverse
        p_ref[rows, cols] = w.astype(BF16)
        ds_ref[rows, cols] = (w * (tile_of(d_ref, first, b) - delta)).astype(BF16)


def interleaved(many, few):
    done = 0
    for i, piece in enumerate(many):
        piece()
        while done < len(few) and (done + 1) * len(many) <= (i + 1) * len(few):
            few[done]()
            done += 1
    assert done == len(few)


def kernel(
    lengths_hbm,
    segments_hbm,
    q_hbm,
    g_hbm,
    branch_hbm,
    root_hbm,
    dq_ref,
    db_ref,
    out_ref,
    lengths,
    segments,
    q_s,
    g_s,
    branch_s,
    root_ref,
    kv,
    sa,
    sb,
    da,
    db,
    pa,
    pb,
    ds_a,
    ds_b,
    q_t,
    g_t,
    acc,
    branch_acc,
    stats,
    dpart,
    r0,
    s1,
    r1,
    s2,
    r2,
    s3,
    r3,
    in_sem,
    z_send,
    z_recv,
    y_send,
    y_recv,
    c_send,
    c_recv,
    s0_send,
    s0_recv,
    s1_send,
    s1_recv,
    s2_send,
    s2_recv,
    s3_send,
    s3_recv,
):
    grp = lax.axis_index("grp")
    dev = lax.axis_index("dev")
    x, z_lo = grp // 2, grp % 2
    y, z_hi, c = dev // 8, (dev // 2) % 4, dev % 2
    z = 2 * z_hi + z_lo

    def at(px, py, pz, pc):
        return (px * 2 + pz % 2, py * 8 + (pz // 2) * 2 + pc)

    def ring_z(offset):
        return (z + offset + NZ) % NZ

    away = 2 * z_lo - 1
    z_dests = [at(x, y, ring_z(away * k), c) for k in (3, 2, 1)]
    y_dests = [at(x, (y + k) % NY, z, c) for k in (2, 1, 3)]
    other_core = at(x, y, z, 1 - c)
    hops = (0, 1, 2, 1)
    farthest_first = sorted(range(1, NX * NY), key=lambda k: -hops[k // NY] - hops[k % NY])
    plane = [((x + k // NY) % NX, (y + k % NY) % NY) for k in farthest_first]
    column = [(z + k) % NZ for k in (4, 3, 5, 2, 6, 1, 7)]
    x_dests = [at((x + k) % NX, y, z, c) for k in (2, 1, 3)]

    q_copies = [pltpu.make_async_copy(q_hbm.at[t], q_s.at[t], in_sem.at[t]) for t in range(2)]
    g_copies = [pltpu.make_async_copy(g_hbm.at[t], g_s.at[t], in_sem.at[2 + t]) for t in range(2)]
    b_copy = pltpu.make_async_copy(branch_hbm, branch_s, in_sem.at[4])
    small = (
        pltpu.make_async_copy(lengths_hbm, lengths, in_sem.at[5]),
        pltpu.make_async_copy(segments_hbm, segments, in_sem.at[6]),
        pltpu.make_async_copy(root_hbm, root_ref, in_sem.at[7]),
    )
    for copy in (*small[::-1], b_copy, q_copies[0], g_copies[0], q_copies[1], g_copies[1]):
        copy.start()

    barrier = pltpu.get_barrier_semaphore()

    def greet(device):
        pl.semaphore_signal(barrier, inc=1, device_id=device, device_id_type=MESH)

    greet(other_core)
    for px, py in plane:
        greet(at(px, py, z, c))
    for pz in column:
        greet(at(x, y, pz, c))
    pl.semaphore_wait(barrier, 1 + len(plane) + len(column))

    def remote(src, dst, send_sem, recv_sem, device):
        return pltpu.make_async_remote_copy(
            src_ref=src,
            dst_ref=dst,
            send_sem=send_sem,
            recv_sem=recv_sem,
            device_id=device,
            device_id_type=MESH,
        )

    def arrived(ref, sem):
        pltpu.make_async_copy(ref, ref, sem).wait()

    def gather_z(chunk):
        start = (chunk % 2) * WIDTH + (chunk // 2) * DH
        src = root_ref.at[:, start : start + DH]
        dst = kv.at[chunk, y, c, z_hi]
        pltpu.make_async_copy(src, dst, z_recv.at[chunk]).start()
        for device in z_dests:
            remote(src, dst, z_send, z_recv.at[chunk], device).start()

    def gather_y(chunk):
        block = kv.at[chunk, y, c]
        arrived(block, z_recv.at[chunk])
        for device in y_dests:
            remote(block, block, y_send, y_recv.at[chunk], device).start()

    def gather_core(chunk):
        arrived(kv.at[chunk, pl.ds(0, 3), c], y_recv.at[chunk])
        block = kv.at[chunk, :, c]
        remote(block, block, c_send, c_recv.at[chunk], other_core).start()

    def gathered(chunk):
        arrived(kv.at[chunk, :, 1 - c], c_recv.at[chunk])

    def reduce_core(head, kind):
        both = pl.ds(2 * kind, 2)
        src, dst = dpart.at[head, :, 1 - c, both], r0.at[head, :, both]
        remote(src, dst, s0_send, s0_recv.at[head], other_core).start()

    def reduce_plane(head):
        arrived(r0.at[head], s0_recv.at[head])
        s1[head] = (dpart[head, :, c].astype(F32) + r0[head].astype(F32)).astype(BF16)
        for k, (px, py) in enumerate(plane):
            remote(
                s1.at[head, py, px], r1.at[head, k], s1_send, s1_recv.at[head], at(px, py, z, c)
            ).start()

    def reduce_column(head):
        arrived(r1.at[head], s1_recv.at[head])
        s2[head] = (s1[head, y, x].astype(F32) + jnp.sum(r1[head].astype(F32), axis=0)).astype(BF16)
        for k, pz in enumerate(column):
            remote(
                s2.at[head, pz // 2], r2.at[head, k], s2_send, s2_recv.at[head], at(x, y, pz, c)
            ).start()

    def share_sum(head):
        arrived(r2.at[head], s2_recv.at[head])
        summed = s2[head, z_hi].astype(F32) + jnp.sum(r2[head].astype(F32), axis=0)
        s3[head] = summed
        r3[head, x] = summed
        for device in x_dests:
            remote(s3.at[head], r3.at[head, x], s3_send, s3_recv.at[head], device).start()

    def reduce_done(head):
        arrived(r3.at[head, pl.ds(0, 3)], s3_recv.at[head])
        for part in range(NX):
            cols = pl.ds(pl.multiple_of((part // 2) * WIDTH + head * DH, DH), DH)
            out_ref[(part % 2) * 16 : (part % 2 + 1) * 16, cols] = r3[head, part]

    ds_s = (ds_a, ds_b)

    def columns(first, count=1):
        return pl.ds(pl.multiple_of(first * DH, DH), count * DH)

    def scores_of(index, pack, s_ref, d_ref):
        head, t = index // 2, index % 2
        live = lax.broadcasted_iota(jnp.int32, (TILE, DH), 0) < lengths[t]
        first = head * GROUP + pack * PACK
        qs = [q_s[t, :, columns(first + j)] for j in range(PACK)]
        gs = [
            jnp.where(live, g_s[t, :, columns(first + j)], jnp.zeros((), BF16)) for j in range(PACK)
        ]
        q, g = jnp.concatenate(qs, axis=0), jnp.concatenate(gs, axis=0)

        def turn():
            for j in range(PACK):
                q_t[pack, :, j * TILE : (j + 1) * TILE] = qs[j].T
                g_t[pack, :, j * TILE : (j + 1) * TILE] = gs[j].T

        def root(of, ref, chunk, b):
            part = kv[chunk, b].reshape(R // SEGS, DH)
            ref[:, b * R // SEGS : (b + 1) * R // SEGS] = dot(of, part, NT)

        def branch(of, ref, start):
            ref[:, R:] = dot(of, branch_s[t, :, columns(start + head)], NT)

        pieces = []
        for of, ref, kind in ((q, s_ref, 0), (g, d_ref, 1)):
            pieces += [functools.partial(root, of, ref, 2 * head + kind, b) for b in range(SEGS)]
            pieces.append(functools.partial(branch, of, ref, kind * KVH))
        return pieces + [turn]

    def key_grads(index, pack, p_ref, is_first):
        part = R // SEGS

        def root(kind, ref, rows_t, b):
            cols = slice(b * part, (b + 1) * part)
            acc[kind, :, cols] = acc[kind, :, cols] + dot(rows_t[pack], ref[:, cols], NN)

        def branch(kind, ref, rows_t):
            term = dot(rows_t[pack], ref[:, R:], NN)
            branch_acc[kind] = term if is_first else branch_acc[kind] + term

        pieces = []
        for kind, ref, rows_t in ((1, p_ref, g_t), (0, ds_s[pack].at[index], q_t)):
            pieces += [functools.partial(root, kind, ref, rows_t, b) for b in range(SEGS)]
            pieces.append(functools.partial(branch, kind, ref, rows_t))
        return pieces

    def softmax_of(index, pack, s_ref, d_ref, p_ref):
        segment = segments[index % 2]
        ds_ref = ds_s[pack].at[index]
        count = PACK * TILE // ROWS

        def piece(i):
            if i + 2 * AHEAD < count:
                peaks((i + 2 * AHEAD) * ROWS, segment, s_ref, stats)
            if 0 <= i + AHEAD < count:
                exponentials((i + AHEAD) * ROWS, segment, s_ref, d_ref, stats)
            if i >= 0:
                weigh(i * ROWS, s_ref, d_ref, p_ref, ds_ref, stats)

        return [functools.partial(piece, i) for i in range(-2 * AHEAD, count)]

    def put_branch(index):
        head, t = index // 2, index % 2
        db_ref[t, :, columns(head)] = (branch_acc[0].T * SCALE).astype(BF16)
        db_ref[t, :, columns(KVH + head)] = branch_acc[1].T.astype(BF16)

    def put_root(head):
        shape = (NY, 2, NZ // 2, 2, 16, DH)
        for kind in (1, 0):
            rows = acc[kind].T
            rows = (rows * SCALE if kind == 0 else rows).astype(BF16).reshape(shape)
            for half in range(2):
                dpart[head, :, :, 2 * kind + half] = rows[:, :, :, half]
            reduce_core(head, kind)
        acc[...] = jnp.zeros_like(acc)

    for copy in small:
        copy.wait()
    for chunk in range(CHUNKS):
        gather_z(chunk)
    for chunk in range(2):
        gather_y(chunk)
    acc[...] = jnp.zeros_like(acc)
    branch_acc[...] = jnp.zeros_like(branch_acc)
    q_t[1] = jnp.zeros_like(q_t[1])
    g_t[1] = jnp.zeros_like(g_t[1])
    pb[...] = jnp.zeros_like(pb)
    ds_b[2 * KVH] = jnp.zeros_like(pb)
    for chunk in range(2):
        gather_core(chunk)
    for chunk in range(2, 4):
        gather_y(chunk)
    b_copy.wait()
    q_copies[0].wait()
    g_copies[0].wait()
    pieces = scores_of(0, 0, sa, da)
    for piece in pieces[SEGS : SEGS + 1] + pieces[2 * SEGS + 1 :]:
        piece()
    gathered(0)
    for piece in pieces[:SEGS]:
        piece()
    gathered(1)
    for piece in pieces[SEGS + 1 : 2 * SEGS + 1]:
        piece()

    def step(index, carry, final=False):
        head, t = index // 2, index % 2
        before = jnp.where(index == 0, 2 * KVH, index - 1)
        after = index + 1

        @pl.when(index == 0)
        def _():
            q_copies[1].wait()
            g_copies[1].wait()
            for chunk in range(4, CHUNKS):
                gather_y(chunk)

        interleaved(
            softmax_of(index, 0, sa, da, pa),
            key_grads(before, 1, pb, False) + scores_of(index, 1, sb, db),
        )

        @pl.when(index > 0)
        def _():
            put_branch(before)

        @pl.when(jnp.logical_and(t == 0, head >= 1))
        def _():
            put_root(head - 1)

        @pl.when(jnp.logical_and(t == 0, head < KVH - 1))
        def _():
            gather_core(2 * head + 2)
            gather_core(2 * head + 3)

        @pl.when(jnp.logical_and(t == 1, head < KVH - 1))
        def _():
            gathered(2 * head + 2)
            gathered(2 * head + 3)

        @pl.when(jnp.logical_and(t == 1, head >= 1))
        def _():
            reduce_plane(head - 1)

        @pl.when(jnp.logical_and(t == 1, head >= 2))
        def _():
            reduce_column(head - 2)

        interleaved(
            softmax_of(index, 1, sb, db, pb),
            key_grads(index, 0, pa, True) + ([] if final else scores_of(after, 0, sa, da)),
        )

        @pl.when(jnp.logical_and(t == 0, head == KVH - 1))
        def _():
            share_sum(head - 3)

        return carry

    def query_grads(index, carry):
        head, t = index // 2, index % 2
        k_cols = pl.ds(pl.multiple_of(head * DH, DH), DH)
        for pack in range(2):
            rows = ds_s[pack].at[index]
            dq = dot(rows[:, :R], kv[2 * head].reshape(R, DH), NN)
            dq = dq + dot(rows[:, R:], branch_s[t, :, k_cols], NN)
            dq = (dq * SCALE).astype(BF16)
            for j in range(PACK):
                cols = columns(head * GROUP + pack * PACK + j)
                dq_ref[t, :, cols] = dq[j * TILE : (j + 1) * TILE]
        return carry

    last = KVH - 1
    lax.fori_loop(0, 2 * KVH - 1, step, 0)
    step(jnp.int32(2 * KVH - 1), 0, final=True)
    for piece in key_grads(2 * KVH - 1, 1, pb, False):
        piece()
    put_root(last)
    put_branch(2 * KVH - 1)
    reduce_column(last - 1)
    lax.fori_loop(0, 1, query_grads, 0)
    reduce_plane(last)
    share_sum(last - 2)
    reduce_done(last - 3)
    lax.fori_loop(1, 5, query_grads, 0)
    share_sum(last - 1)
    reduce_column(last)
    reduce_done(last - 2)
    lax.fori_loop(5, 8, query_grads, 0)
    reduce_done(last - 1)
    share_sum(last)
    reduce_done(last)

    for _ in range(3):
        arrived(kv.at[:, 0, 0, 0], z_send)
        arrived(kv.at[:, 0, 0], y_send)
    arrived(kv.at[:, :, 0], c_send)
    arrived(r0, s0_send)
    arrived(r1, s1_send)
    arrived(r2, s2_send)
    arrived(r3.at[:, pl.ds(0, 3)], s3_send)


def local(query, grad_out, branch_kv, root_kv, lengths, segments):
    rows = R // 32
    hbm = pl.BlockSpec(memory_space=pltpu.HBM)
    vmem = pl.BlockSpec(memory_space=pltpu.VMEM)
    dma = pltpu.SemaphoreType.DMA
    blocks = (CHUNKS, NY, 2, NZ // 2, rows, DH)
    half = (KVH, NY, NX, NZ // 2, 16, DH)
    return pl.pallas_call(
        kernel,
        out_shape=(
            jax.ShapeDtypeStruct(query.shape, BF16),
            jax.ShapeDtypeStruct(branch_kv.shape, BF16),
            jax.ShapeDtypeStruct(root_kv.shape, F32),
        ),
        in_specs=[hbm] * 6,
        out_specs=(vmem, vmem, vmem),
        scratch_shapes=[
            pltpu.SMEM(lengths.shape, jnp.int32),
            pltpu.SMEM(segments.shape, jnp.int32),
            pltpu.VMEM(query.shape, BF16),
            pltpu.VMEM(query.shape, BF16),
            pltpu.VMEM(branch_kv.shape, BF16),
            pltpu.VMEM(root_kv.shape, BF16),
            pltpu.VMEM(blocks, BF16),
            *[pltpu.VMEM((PACK * TILE, R + TILE), F32)] * 4,
            *[pltpu.VMEM((PACK * TILE, R + TILE), BF16)] * 2,
            *[pltpu.VMEM((2 * KVH + 1, PACK * TILE, R + TILE), BF16)] * 2,
            pltpu.VMEM((2, DH, PACK * TILE), BF16),
            pltpu.VMEM((2, DH, PACK * TILE), BF16),
            pltpu.VMEM((2, DH, R), F32),
            pltpu.VMEM((2, DH, TILE), F32),
            pltpu.VMEM((3, PACK * TILE, DH), F32),
            pltpu.VMEM((KVH, NY, 2, NX, NZ // 2, 16, DH), BF16),
            pltpu.VMEM(half, BF16),
            pltpu.VMEM(half, BF16),
            pltpu.VMEM((KVH, NX * NY - 1, NZ // 2, 16, DH), BF16),
            pltpu.VMEM((KVH, NZ // 2, 16, DH), BF16),
            pltpu.VMEM((KVH, NZ - 1, 16, DH), BF16),
            pltpu.VMEM((KVH, 16, DH), F32),
            pltpu.VMEM((KVH, NX, 16, DH), F32),
            dma((8,)),
            dma,
            dma((CHUNKS,)),
            dma,
            dma((CHUNKS,)),
            dma,
            dma((CHUNKS,)),
            dma,
            dma((KVH,)),
            dma,
            dma((KVH,)),
            dma,
            dma((KVH,)),
            dma,
            dma((KVH,)),
        ],
        compiler_params=pltpu.CompilerParams(
            collective_id=0, has_side_effects=True, vmem_limit_bytes=49 << 20
        ),
    )(*[pltpu.with_memory_space_constraint(a, pltpu.HBM) for a in (lengths, segments, query, grad_out, branch_kv, root_kv)])


def solution(mesh):
    placed = (
        P(("grp", "dev"), None, None),
        P(("grp", "dev"), None, None),
        P(("grp", "dev"), None, None),
        P("dev", None),
        P(("grp", "dev")),
        P(("grp", "dev")),
    )
    return jax.shard_map(
        local,
        mesh=mesh,
        in_specs=placed,
        out_specs=(P(("grp", "dev"), None, None), P(("grp", "dev"), None, None), P("dev", None)),
        check_vma=False,
    )
```
